128 devices in a mesh: grp: 8 (over y, core), nbr: 16 (over x, z).
Axes of the slice: x: 4, y: 4, z: 4, core: 2. Of those that a mesh axis runs over, the one named last changes fastest.
Arguments:
- sims: float32 [2048, 128, 128], P(('grp', 'nbr')), may hold values from -6 to 6
- own_tiles: float32 [24576, 128, 128], P(('grp', 'nbr')), may hold values from -0.15625 to 0.15625
- own_cols: int32 [24576], P(('grp', 'nbr')), may hold values from 0 to 271
- own_rows: int32 [24576], P(('grp', 'nbr')), may hold values from 0 to 15
- help_tiles: float32 [4096, 128, 128], P(('grp', 'nbr')), may hold values from -0.15625 to 0.15625
- help_cols: int32 [4096], P(('grp', 'nbr')), may hold values from 0 to 271
- help_rows: int32 [4096], P(('grp', 'nbr')), may hold values from 0 to 15
- help_live: int32 [4096], P(('grp', 'nbr')), may hold values from 0 to 1, as said below
Outputs:
- reobserved: float32 [2048, 128, 128], P(('grp', 'nbr'))
The draws below stay inside these ranges and needn't reach their ends.
Inputs may be any that keep to these rules, and one draw needn't show every extreme that they name: `help_live`: helper slot j of a device serves the owner of neighbour index j // 2 in the same group, so at most 2 live slots go from one device to one owner; in every group one owner receives all 2 slots live from every device of the group.
All inputs are finite; a program needn't handle non-finite values.
Results may differ from the reference program's by a relative error of at most 0.0001.
Values sent between devices are 32-bit elements; how exact they have to be, the bound alone decides.
A program may use at most 192 MiB of HBM per device.

```python
import jax
import jax.numpy as jnp
from jax import lax

TILE = 128
SIMS = 128
ROWS_DEV = 16
TILES_ROW = 12
CAP = 2
RIM = 8
GROUP_ROWS = 256
BLOCKS = 2048
HELP_DEV = 32
N_GRP = 8
N_NBR = 16


def draw_help_live(key, part):
    devices = N_GRP * N_NBR
    base = jax.random.fold_in(key, 7)
    key_bits, key_owner = jax.random.split(base)
    bits = jax.random.randint(key_bits, (devices, N_NBR, CAP), 0, 2).astype(jnp.int32)
    chosen = jax.random.randint(key_owner, (N_GRP,), 0, N_NBR).astype(jnp.int32)
    forced = (jnp.arange(N_NBR, dtype=jnp.int32)[None, :] == chosen[:, None]).astype(jnp.int32)
    forced = jnp.repeat(forced, N_NBR, axis=0)
    live = jnp.maximum(bits, forced[:, :, None])
    return live.reshape(-1).astype(jnp.int32)


def touch_ends(entries, rng, smallest, largest):
    longest = entries.shape.index(max(entries.shape))
    spots = []
    for shift in (0, 1):
        where = [jax.random.randint(jax.random.fold_in(rng, axis), (), 0, length) for axis, length in enumerate(entries.shape)]
        where[longest] = (where[longest] + shift) % entries.shape[longest]
        spots.append(tuple(where))
    return entries.at[spots[0]].set(smallest).at[spots[1]].set(largest)


def shard_levels(key, dims, pieces, least, high):
    loudness = 1.0
    for position, blocks in pieces:
        heights = jax.random.uniform(jax.random.fold_in(jax.random.fold_in(key, 6), position), (blocks,), jnp.float32, least / len(pieces), high / len(pieces))
        loudness = loudness * jnp.repeat(jnp.exp(heights), dims[position] // blocks).reshape((-1,) + (1,) * (len(dims) - 1 - position))
    return loudness


def gaussian(stream_key, extent, scale, most, cuts=(), kind=jnp.bfloat16):
    values = scale * jax.random.normal(stream_key, extent, jnp.float32)
    if cuts:
        values = values * shard_levels(stream_key, extent, cuts, -0.22, 0.18)
    return jnp.clip(values, -most, most).astype(kind)


def setup_inputs(seed: int = 0) -> dict:
    arg_keys = jax.random.split(jax.random.key(seed), 9)
    return {
        "sims": gaussian(arg_keys[0], (BLOCKS, TILE, SIMS), 1.0, 6.0, ((0, 128),), jnp.float32),
        "own_tiles": gaussian(arg_keys[1], (BLOCKS * TILES_ROW, TILE, TILE), (TILE * TILES_ROW) ** -0.5, 0.15625, ((0, 128),), jnp.float32),
        "own_cols": touch_ends(jax.random.randint(arg_keys[2], (BLOCKS * TILES_ROW,), 0, GROUP_ROWS + 2 * RIM), jax.random.fold_in(arg_keys[2], 1), 0, (GROUP_ROWS + 2 * RIM) - 1).astype(jnp.int32),
        "own_rows": touch_ends(jax.random.randint(arg_keys[3], (BLOCKS * TILES_ROW,), 0, ROWS_DEV), jax.random.fold_in(arg_keys[3], 1), 0, ROWS_DEV - 1).astype(jnp.int32),
        "help_tiles": gaussian(arg_keys[4], (BLOCKS // ROWS_DEV * HELP_DEV, TILE, TILE), (TILE * TILES_ROW) ** -0.5, 0.15625, ((0, 128),), jnp.float32),
        "help_cols": touch_ends(jax.random.randint(arg_keys[5], (BLOCKS // ROWS_DEV * HELP_DEV,), 0, GROUP_ROWS + 2 * RIM), jax.random.fold_in(arg_keys[5], 1), 0, (GROUP_ROWS + 2 * RIM) - 1).astype(jnp.int32),
        "help_rows": touch_ends(jax.random.randint(arg_keys[6], (BLOCKS // ROWS_DEV * HELP_DEV,), 0, ROWS_DEV), jax.random.fold_in(arg_keys[6], 1), 0, ROWS_DEV - 1).astype(jnp.int32),
        "help_live": draw_help_live(jax.random.fold_in(arg_keys[8], 71), 0),
    }


def reference(sims, own_tiles, own_cols, own_rows, help_tiles, help_cols, help_rows, help_live):
    devices = N_GRP * N_NBR
    group_rows = ROWS_DEV * N_NBR
    tile_dev = ROWS_DEV * TILES_ROW
    help_dev = N_NBR * CAP
    padded = jnp.pad(sims, ((RIM, RIM), (0, 0), (0, 0)))
    high = lax.Precision.HIGHEST

    def visit(device, total):
        group = device // N_NBR
        extended = lax.dynamic_slice_in_dim(padded, (group * group_rows).astype(jnp.int32), group_rows + 2 * RIM, 0)
        tiles = lax.dynamic_slice_in_dim(own_tiles, (device * tile_dev).astype(jnp.int32), tile_dev, 0)
        cols = lax.dynamic_slice_in_dim(own_cols, (device * tile_dev).astype(jnp.int32), tile_dev, 0)
        rows = lax.dynamic_slice_in_dim(own_rows, (device * tile_dev).astype(jnp.int32), tile_dev, 0)
        picked = jnp.take(extended, cols, axis=0)
        terms = jnp.einsum("tij,tjs->tis", tiles, picked, precision=high)
        select = (rows[None, :] == jnp.arange(ROWS_DEV, dtype=jnp.int32)[:, None]).astype(jnp.float32)
        own_sum = jnp.einsum("rt,tis->ris", select, terms, precision=high)
        start = (device * ROWS_DEV).astype(jnp.int32)
        block = lax.dynamic_slice_in_dim(total, start, ROWS_DEV, 0)
        total = lax.dynamic_update_slice_in_dim(total, block + own_sum, start, 0)
        htiles = lax.dynamic_slice_in_dim(help_tiles, (device * help_dev).astype(jnp.int32), help_dev, 0)
        hcols = lax.dynamic_slice_in_dim(help_cols, (device * help_dev).astype(jnp.int32), help_dev, 0)
        hrows = lax.dynamic_slice_in_dim(help_rows, (device * help_dev).astype(jnp.int32), help_dev, 0)
        hlive = lax.dynamic_slice_in_dim(help_live, (device * help_dev).astype(jnp.int32), help_dev, 0)
        hpicked = jnp.take(extended, hcols, axis=0)
        hterms = jnp.einsum("tij,tjs->tis", htiles, hpicked, precision=high)
        hterms = hterms * hlive.astype(jnp.float32)[:, None, None]
        target = (jnp.arange(help_dev, dtype=jnp.int32) // CAP) * ROWS_DEV + hrows
        hselect = (target[None, :] == jnp.arange(group_rows, dtype=jnp.int32)[:, None]).astype(jnp.float32)
        help_sum = jnp.einsum("rt,tis->ris", hselect, hterms, precision=high)
        gstart = (group * group_rows).astype(jnp.int32)
        gblock = lax.dynamic_slice_in_dim(total, gstart, group_rows, 0)
        return lax.dynamic_update_slice_in_dim(total, gblock + help_sum, gstart, 0)

    total = jnp.zeros(sims.shape, jnp.float32)
    return lax.fori_loop(0, devices, visit, total)
```

```python
import functools

import jax
import jax.numpy as jnp
from jax import lax
from jax.experimental import pallas as pl
from jax.experimental.pallas import tpu as pltpu
from jax.sharding import PartitionSpec as P

RIM = 8
UNIT = 4
SIDE = 4
DEPTH = 8
MESH = pl.DeviceIdType.MESH


def unit_id(origin, sub):
    return ((origin[0] % SIDE) * SIDE + origin[1] % SIDE) * 4 + sub


def gather_queues():
    queues = []
    for axis in (0, 1):
        for way in (1, -1):
            near, far = ((0, 1), (2, 3)) if axis == 0 else ((2, 3), (0, 1))
            if way < 0:
                near, far = near[::-1], far[::-1]

            def at(along, across, axis=axis):
                return (along, across) if axis == 0 else (across, along)

            queue = [
                (at(0, 0), near[0]),
                (at(0, 0), near[1]),
                (at(0, 0), far[0]),
                (at(-way, 0), near[0]),
                (at(0, 0), far[1]),
                (at(0, -1), far[0]),
                (at(0, 1), far[0]),
                (at(0, -1), far[1]),
                (at(0, 1), far[1]),
                (at(0, 2), far[0]),
                (at(0, 2), far[1]),
                (at(-way, 0), far[0]),
                (at(-way, -1), far[0]),
                (at(-way, 1), far[0]),
                (at(-way, 2), far[0]),
            ]
            queues.append((axis, way, queue))
    return queues


class Link:
    def __init__(self, send, recv):
        self.send, self.recv, self.sent = send, recv, []

    def start(self, src, dst, arrival, device):
        copy = pltpu.make_async_remote_copy(
            src_ref=src,
            dst_ref=dst,
            send_sem=self.send.at[len(self.sent)],
            recv_sem=self.recv.at[arrival],
            device_id=device,
            device_id_type=MESH,
        )
        copy.start()
        self.sent.append(copy)

    def arrive(self, dst, arrival, device):
        pltpu.make_async_remote_copy(
            src_ref=dst,
            dst_ref=dst,
            send_sem=self.send.at[0],
            recv_sem=self.recv.at[arrival],
            device_id=device,
            device_id_type=MESH,
        ).wait_recv()


def exchange(
    sims, helps, meta, ext_out, tiles_out, meta_out,
    ext, first, passing, second, metas,
    send, recv, rim_send, rim_recv, local_sem,
):
    n, g = lax.axis_index("nbr"), lax.axis_index("grp")
    groups = lax.axis_size("grp")
    x, z = n // SIDE, lax.rem(n, SIDE)
    blocks = sims.shape[0]
    total = ext.shape[0]

    def place(origin):
        return lax.rem(x + origin[0] + SIDE, SIDE) * SIDE + lax.rem(z + origin[1] + SIDE, SIDE)

    def step(axis, way):
        return (way, 0) if axis == 0 else (0, way)

    def neighbour(axis, way):
        return {"nbr": place(step(axis, way))}

    barrier = pltpu.get_barrier_semaphore()
    for axis in (0, 1):
        for way in (1, -1):
            pl.semaphore_signal(barrier, inc=1, device_id=neighbour(axis, way), device_id_type=MESH)

    @pl.when(g > 0)
    def _():
        pl.semaphore_signal(barrier, inc=1, device_id={"grp": g - 1}, device_id_type=MESH)

    @pl.when(g < groups - 1)
    def _():
        pl.semaphore_signal(barrier, inc=1, device_id={"grp": g + 1}, device_id_type=MESH)

    mine = pltpu.make_async_copy(sims, ext.at[pl.ds(RIM + n * blocks, blocks)], local_sem.at[0])
    mine.start()
    note = pltpu.make_async_copy(meta, metas.at[n], local_sem.at[1])
    note.start()
    bundles = [
        pltpu.make_async_copy(helps.at[x, :, 0], first.at[0, 0], local_sem.at[2]),
        pltpu.make_async_copy(helps.at[:, z, 1], first.at[1, 0], local_sem.at[3]),
    ]
    for bundle in bundles:
        bundle.start()

    @pl.when(g == 0)
    def _():
        ext[:RIM] = jnp.zeros((RIM,) + ext.shape[1:], ext.dtype)

    @pl.when(g == groups - 1)
    def _():
        ext[total - RIM :] = jnp.zeros((RIM,) + ext.shape[1:], ext.dtype)

    pl.semaphore_wait(
        barrier, 4 + (g > 0).astype(jnp.int32) + (g < groups - 1).astype(jnp.int32)
    )
    mine.wait()
    note.wait()
    link = Link(send, recv)

    def quarter(origin, sub):
        return ext.at[pl.ds(RIM + place(origin) * blocks + sub * UNIT, UNIT)]

    here = {unit_id((0, 0), sub) for sub in range(4)}

    def need(origin, sub):
        name = unit_id(origin, sub)
        if name not in here:
            here.add(name)
            link.arrive(quarter(origin, sub), name, neighbour(0, 1))

    queues = gather_queues()
    base = 64

    def note_row(dx):
        return metas.at[lax.rem(x + dx + SIDE, SIDE) * SIDE + z]

    def note_wait(ref, arrival):
        link.arrive(ref, arrival, neighbour(0, 1))

    for turn in range(len(queues[0][2])):
        for axis, way, queue in queues:
            origin, sub = queue[turn]
            need(origin, sub)
            seen = (origin[0] - step(axis, way)[0], origin[1] - step(axis, way)[1])
            link.start(
                quarter(origin, sub), quarter(origin, sub), unit_id(seen, sub), neighbour(axis, way)
            )
        if turn == 0:
            link.start(note_row(0), note_row(0), base, neighbour(0, 1))
            link.start(note_row(0), note_row(0), base + 1, neighbour(0, -1))
        if turn == 3:
            note_wait(note_row(-1), base)
            note_wait(note_row(1), base + 1)
            link.start(note_row(-1), note_row(-1), base + 2, neighbour(0, 1))
        if turn == 6:
            note_wait(note_row(2), base + 2)
            for dx in range(SIDE):
                link.start(note_row(dx), note_row(dx), base + 3 + dx, neighbour(1, 1))
                link.start(note_row(dx), note_row(dx), base + 7 + dx, neighbour(1, -1))
        if turn == 9:
            for dx in range(SIDE):
                behind = metas.at[place((dx, -1))]
                note_wait(behind, base + 3 + dx)
                note_wait(metas.at[place((dx, 1))], base + 7 + dx)
                link.start(behind, behind, base + 11 + dx, neighbour(1, 1))
    for dx in range(SIDE):
        note_wait(metas.at[place((dx, 2))], base + 11 + dx)
    base += 15
    for bundle in bundles:
        bundle.wait()

    def bundle_of(slot, to):
        at = place(to)
        return helps.at[at // SIDE, :, 0] if slot == 0 else helps.at[:, lax.rem(at, SIDE), 1]

    def pair_of(slot, to, low):
        at = place(to)
        part = pl.ds(low, 2)
        return helps.at[at // SIDE, part, 0] if slot == 0 else helps.at[part, lax.rem(at, SIDE), 1]

    def final(slot, along, across):
        dx, dz = (along % SIDE, across % SIDE) if slot == 0 else (across % SIDE, along % SIDE)
        return tiles_out.at[slot, dx, dz]

    def arrival(slot, kind):
        return base + slot * 28 + kind

    def target(slot, way):
        axis = 1 - slot
        at = place(step(axis, way))
        return lax.rem(at, SIDE) if axis == 1 else at // SIDE

    def opening(slot):
        for way, low in ((1, 0), (-1, 2)):
            k = 0 if way > 0 else 1
            link.start(
                pair_of(slot, step(slot, 2), low), passing.at[slot, k], arrival(slot, k),
                neighbour(slot, way),
            )
            link.start(
                bundle_of(slot, step(slot, way)), first.at[slot, -way % SIDE],
                arrival(slot, 2 + k), neighbour(slot, way),
            )

    def relay(slot):
        for way, low in ((1, 0), (-1, 2)):
            k = 0 if way > 0 else 1
            note_wait(passing.at[slot, k], arrival(slot, k))
            link.start(
                passing.at[slot, k], first.at[slot, 2, pl.ds(low, 2)], arrival(slot, 4 + k),
                neighbour(slot, way),
            )

    def direct(slot, along):
        for way in (1, -1):
            link.start(
                first.at[slot, along % SIDE, target(slot, way)], final(slot, along, -way),
                arrival(slot, 6 + (along % SIDE) * 4 + (-way) % SIDE), neighbour(1 - slot, way),
            )

    by = {0: 1, 1: 1, 3: -1, 2: -1}

    def detour(slot, along):
        way = by[along % SIDE]
        link.start(
            first.at[slot, along % SIDE, target(slot, 2)], second.at[slot, along % SIDE],
            arrival(slot, 22 + along % SIDE), neighbour(1 - slot, way),
        )

    def hand_on(slot, along):
        way = by[along % SIDE]
        note_wait(second.at[slot, along % SIDE], arrival(slot, 22 + along % SIDE))
        link.start(
            second.at[slot, along % SIDE], final(slot, along, 2),
            arrival(slot, 6 + (along % SIDE) * 4 + 2), neighbour(1 - slot, way),
        )

    def bundle_wait(slot, way):
        k = 0 if way > 0 else 1
        note_wait(first.at[slot, -way % SIDE], arrival(slot, 2 + k))

    slots = (0, 1)
    for slot in slots:
        opening(slot)
    for slot in slots:
        detour(slot, 0)
        direct(slot, 0)

    for a in range(SIDE):
        for b in range(SIDE):
            for sub in range(4):
                need((a, b), sub)
    up = pltpu.make_async_remote_copy(
        src_ref=ext.at[pl.ds(total - 2 * RIM, RIM)], dst_ref=ext.at[pl.ds(0, RIM)],
        send_sem=rim_send.at[0], recv_sem=rim_recv.at[0],
        device_id={"grp": lax.rem(g + 1, groups)}, device_id_type=MESH,
    )
    down = pltpu.make_async_remote_copy(
        src_ref=ext.at[pl.ds(RIM, RIM)], dst_ref=ext.at[pl.ds(total - RIM, RIM)],
        send_sem=rim_send.at[1], recv_sem=rim_recv.at[1],
        device_id={"grp": lax.rem(g + groups - 1, groups)}, device_id_type=MESH,
    )

    @pl.when(g < groups - 1)
    def _():
        up.start()

    @pl.when(g > 0)
    def _():
        down.start()

    for slot in slots:
        relay(slot)
    for slot in slots:
        for way in (1, -1):
            bundle_wait(slot, way)
    for slot in slots:
        direct(slot, -1)
        direct(slot, 1)
        detour(slot, 1)
        detour(slot, -1)

    @pl.when(g > 0)
    def _():
        up.wait_recv()

    @pl.when(g < groups - 1)
    def _():
        down.wait_recv()

    out = pltpu.make_async_copy(ext, ext_out, local_sem.at[0])
    out.start()
    notes = pltpu.make_async_copy(metas, meta_out, local_sem.at[1])
    notes.start()
    for slot in slots:
        hand_on(slot, 0)
        for k, low in ((0, 0), (1, 2)):
            note_wait(first.at[slot, 2, pl.ds(low, 2)], arrival(slot, 4 + k))
        detour(slot, 2)
        direct(slot, 2)
    stay = [
        pltpu.make_async_copy(first.at[0, :, z], tiles_out.at[0, :, 0], local_sem.at[2]),
        pltpu.make_async_copy(first.at[1, :, x], tiles_out.at[1, 0, :], local_sem.at[3]),
    ]
    for copy in stay:
        copy.start()
    for slot in slots:
        hand_on(slot, 1)
        hand_on(slot, -1)
    for slot in slots:
        hand_on(slot, 2)
    for slot in slots:
        for along in range(SIDE):
            for across in (1, 2, 3):
                note_wait(final(slot, along, across), arrival(slot, 6 + along * 4 + across))
    for copy in link.sent:
        copy.wait_send()

    @pl.when(g < groups - 1)
    def _():
        up.wait_send()

    @pl.when(g > 0)
    def _():
        down.wait_send()

    out.wait()
    notes.wait()
    for copy in stay:
        copy.wait()


def split(value):
    high = value.astype(jnp.bfloat16)
    return high, (value - high.astype(jnp.float32)).astype(jnp.bfloat16)


def product(tile, block):
    tile_parts = jnp.concatenate(split(tile), axis=1)
    block_parts = jnp.concatenate(split(block), axis=1)
    both = jnp.dot(
        tile_parts, jnp.concatenate([block_parts, block_parts], axis=0),
        preferred_element_type=jnp.float32,
    )
    return both[:, : block.shape[1]] + both[:, block.shape[1] :]


def products(
    own_cols, own_rows, notes, ext, own_tiles, help_tiles, total, tiles, blocks, tile_sem, block_sem
):
    n = lax.axis_index("nbr")
    x, z = n // SIDE, lax.rem(n, SIDE)
    n_own, n_help = own_tiles.shape[0], help_tiles.shape[0]
    total[...] = jnp.zeros_like(total)

    def copies(src, index, col):
        at = lax.rem(index, DEPTH)
        return (
            pltpu.make_async_copy(src.at[index], tiles.at[at], tile_sem.at[at]),
            pltpu.make_async_copy(ext.at[col], blocks.at[at], block_sem.at[at]),
        )

    def run(count, src, of):
        def fetch(index):
            col, _, live = of(index)

            @pl.when(live > 0)
            def _():
                for copy in copies(src, index, col):
                    copy.start()

        for index in range(DEPTH - 1):
            fetch(index)

        @pl.loop(0, count)
        def _(index):
            @pl.when(index + DEPTH - 1 < count)
            def _():
                fetch(index + DEPTH - 1)

            col, row, live = of(index)

            @pl.when(live > 0)
            def _():
                for copy in copies(src, index, col):
                    copy.wait()
                at = lax.rem(index, DEPTH)
                total[row] += product(tiles[at], blocks[at])

    def own(index):
        return own_cols[index], own_rows[index], 1

    def helper(index):
        slot, dx, dz = index // 16, lax.rem(index // SIDE, SIDE), lax.rem(index, SIDE)
        source = lax.rem(x + dx, SIDE) * SIDE + lax.rem(z + dz, SIDE)
        at = n * 2 + slot
        return notes[source, 0, at], notes[source, 1, at], notes[source, 2, at]

    run(n_own, own_tiles, own)
    run(n_help, help_tiles, helper)


def local(sims, own_tiles, own_cols, own_rows, help_tiles, help_cols, help_rows, help_live):
    blocks, size = sims.shape[0], sims.shape[1:]
    neighbours = lax.axis_size("nbr")
    helps = help_tiles.shape[0]
    extended = blocks * neighbours + 2 * RIM
    any_space = pl.BlockSpec(memory_space=pl.ANY)
    smem = pl.BlockSpec(memory_space=pltpu.SMEM)
    meta = jnp.pad(
        jnp.stack([help_cols, help_rows, help_live]), ((0, 5), (0, 128 - helps))
    )
    ext, tiles, notes = pl.pallas_call(
        exchange,
        out_shape=(
            jax.ShapeDtypeStruct((extended,) + size, jnp.float32),
            jax.ShapeDtypeStruct((2, SIDE, SIDE) + size, jnp.float32),
            jax.ShapeDtypeStruct((neighbours, 8, 128), jnp.int32),
        ),
        in_specs=[any_space] * 3,
        out_specs=(any_space,) * 3,
        scratch_shapes=[
            pltpu.VMEM((extended,) + size, jnp.float32),
            pltpu.VMEM((2, SIDE, SIDE) + size, jnp.float32),
            pltpu.VMEM((2, 2, 2) + size, jnp.float32),
            pltpu.VMEM((2, SIDE) + size, jnp.float32),
            pltpu.VMEM((neighbours, 8, 128), jnp.int32),
            pltpu.SemaphoreType.DMA((160,)),
            pltpu.SemaphoreType.DMA((160,)),
            pltpu.SemaphoreType.DMA((2,)),
            pltpu.SemaphoreType.DMA((2,)),
            pltpu.SemaphoreType.DMA((4,)),
        ],
        compiler_params=pltpu.CompilerParams(
            collective_id=0, has_side_effects=True, vmem_limit_bytes=56 * 2**20
        ),
        name="exchange",
    )(sims, help_tiles.reshape((SIDE, SIDE, 2) + size), meta)
    return pl.pallas_call(
        products,
        out_shape=jax.ShapeDtypeStruct(sims.shape, jnp.float32),
        in_specs=[smem] * 3 + [any_space] * 3,
        out_specs=pl.BlockSpec(memory_space=pltpu.VMEM),
        scratch_shapes=[
            pltpu.VMEM((DEPTH,) + size, jnp.float32),
            pltpu.VMEM((DEPTH,) + size, jnp.float32),
            pltpu.SemaphoreType.DMA((DEPTH,)),
            pltpu.SemaphoreType.DMA((DEPTH,)),
        ],
        name="products",
    )(own_cols, own_rows, notes, ext, own_tiles, tiles.reshape((helps,) + size))


def solution(mesh):
    whole, flat = P(("grp", "nbr"), None, None), P(("grp", "nbr"))
    placed = (whole, whole, flat, flat, whole, flat, flat, flat)
    return jax.shard_map(local, mesh=mesh, in_specs=placed, out_specs=whole, check_vma=False)
```

```python
import jax
import jax.numpy as jnp
from jax import lax
from jax.experimental import pallas as pl
from jax.experimental.pallas import tpu as pltpu
from jax.sharding import PartitionSpec as P

RIM = 8
UNIT = 4
SIDE = 4
UNROLL = 4
MESH = pl.DeviceIdType.MESH


def unit_id(origin, sub):
    return ((origin[0] % SIDE) * SIDE + origin[1] % SIDE) * 4 + sub


def gather_queues():
    queues = []
    for axis in (0, 1):
        for way in (1, -1):
            near, far = ((0, 1), (2, 3)) if axis == 0 else ((2, 3), (0, 1))
            if way < 0:
                near, far = near[::-1], far[::-1]

            def at(along, across, axis=axis):
                return (along, across) if axis == 0 else (across, along)

            queue = [
                (at(0, 0), near[0]),
                (at(0, 0), near[1]),
                (at(0, 0), far[0]),
                (at(-way, 0), near[0]),
                (at(0, 0), far[1]),
                (at(0, -1), far[0]),
                (at(0, 1), far[0]),
                (at(0, -1), far[1]),
                (at(0, 1), far[1]),
                (at(0, 2), far[0]),
                (at(0, 2), far[1]),
                (at(-way, 0), far[0]),
                (at(-way, -1), far[0]),
                (at(-way, 1), far[0]),
                (at(-way, 2), far[0]),
            ]
            queues.append((axis, way, queue))
    return queues


class Link:
    def __init__(self, send, recv):
        self.send, self.recv, self.sent = send, recv, []

    def start(self, src, dst, arrival, device):
        copy = pltpu.make_async_remote_copy(
            src_ref=src,
            dst_ref=dst,
            send_sem=self.send.at[len(self.sent)],
            recv_sem=self.recv.at[arrival],
            device_id=device,
            device_id_type=MESH,
        )
        copy.start()
        self.sent.append(copy)

    def arrive(self, dst, arrival, device):
        pltpu.make_async_remote_copy(
            src_ref=dst,
            dst_ref=dst,
            send_sem=self.send.at[0],
            recv_sem=self.recv.at[arrival],
            device_id=device,
            device_id_type=MESH,
        ).wait_recv()


def split(value):
    high = value.astype(jnp.bfloat16)
    low = (value - high.astype(jnp.float32)).astype(jnp.bfloat16)
    return jnp.concatenate([high, low], axis=1)


def product(tile, block):
    both = jnp.dot(
        tile, jnp.concatenate([block, block], axis=0), preferred_element_type=jnp.float32
    )
    half = both.shape[1] // 2
    return both[:, :half] + both[:, half:]


def order_table(cols, rows, table):
    count = rows.shape[1]
    table[...] = jnp.zeros_like(table)
    line = lax.broadcasted_iota(jnp.int32, (count, count), 1)
    deep = lax.broadcasted_iota(jnp.int32, (count, count), 0)

    def upright(value):
        return jnp.sum(jnp.where(line == deep, value, 0), axis=1, keepdims=True)

    key = rows * 256 + line[:1]
    key_up, col_up = upright(key), upright(cols)
    row_up = jnp.right_shift(key_up, 8)
    rank = jnp.sum((key < key_up).astype(jnp.int32), axis=1, keepdims=True)
    here = rank == line
    before = rank == line - 1
    row_at = jnp.sum(jnp.where(here, row_up, 0), axis=0, keepdims=True)
    row_before = jnp.sum(jnp.where(before, row_up + 1, 0), axis=0, keepdims=True) - 1
    table[0:1, :count] = jnp.sum(jnp.where(here, deep, 0), axis=0, keepdims=True)
    table[1:2, :count] = jnp.sum(jnp.where(here, col_up, 0), axis=0, keepdims=True)
    table[2:3, :count] = (row_at == row_before).astype(jnp.int32)
    upto = jnp.sum((row_up <= line).astype(jnp.int32), axis=0, keepdims=True)
    table[3:4, :count] = jnp.maximum(upto - 1, 0)
    table[4:5, :count] = jnp.minimum(
        jnp.sum((row_up == line).astype(jnp.int32), axis=0, keepdims=True), 1
    )


HELP_ORDER = (
    [(0, 0), (1, 0), (3, 0), (0, 1), (0, 3), (2, 0)]
    + [(1, 1), (1, 3), (3, 1), (3, 3), (0, 2), (1, 2), (3, 2)]
    + [(2, 1), (2, 3), (2, 2)]
)


def exchange(
    sims, helps, tiles, own_cols, own_rows, help_cols, help_rows, help_live,
    sums_out, terms_out, notes_out,
    ext, ext_parts, tile_parts, stage, first, passing, second, arrived, terms, sums,
    metas, vec, table, order, notes,
    send, recv, rim_send, rim_recv, local_sem, stage_sem,
):
    n, g = lax.axis_index("nbr"), lax.axis_index("grp")
    groups = lax.axis_size("grp")
    x, z = n // SIDE, lax.rem(n, SIDE)
    blocks = sims.shape[0]
    total = ext.shape[0]
    n_own = tiles.shape[0]
    last = SIDE * SIDE - 1

    def place(origin):
        return lax.rem(x + origin[0] + SIDE, SIDE) * SIDE + lax.rem(z + origin[1] + SIDE, SIDE)

    def step(axis, way):
        return (way, 0) if axis == 0 else (0, way)

    def neighbour(axis, way):
        return {"nbr": place(step(axis, way))}

    barrier = pltpu.get_barrier_semaphore()
    for axis in (0, 1):
        for way in (1, -1):
            pl.semaphore_signal(barrier, inc=1, device_id=neighbour(axis, way), device_id_type=MESH)

    @pl.when(g > 0)
    def _():
        pl.semaphore_signal(barrier, inc=1, device_id={"grp": g - 1}, device_id_type=MESH)

    @pl.when(g < groups - 1)
    def _():
        pl.semaphore_signal(barrier, inc=1, device_id={"grp": g + 1}, device_id_type=MESH)

    def fetch(src, dst, k):
        copy = pltpu.make_async_copy(src, dst, local_sem.at[k])
        copy.start()
        return copy

    mine = fetch(sims, ext.at[pl.ds(RIM + n * blocks, blocks)], 0)
    told = [
        fetch(ref, metas.at[n, k], 1 + k) for k, ref in enumerate((help_cols, help_rows, help_live))
    ]
    bundles = [
        fetch(helps.at[x, :, 0], first.at[0, 0], 4), fetch(helps.at[:, z, 1], first.at[1, 0], 5)
    ]
    vectors = [fetch(own_cols, vec.at[0], 6), fetch(own_rows, vec.at[1], 7)]

    def load(chunk):
        at = lax.rem(chunk, 2)
        return pltpu.make_async_copy(
            tiles.at[pl.ds(chunk * UNIT, UNIT)], stage.at[at], stage_sem.at[at]
        )

    for chunk in (0, 1):
        load(chunk).start()

    pl.semaphore_wait(
        barrier, 4 + (g > 0).astype(jnp.int32) + (g < groups - 1).astype(jnp.int32)
    )
    mine.wait()
    for copy in told:
        copy.wait()
    link = Link(send, recv)

    def split_unit(start):
        @pl.loop(0, UNIT)
        def _(k):
            ext_parts[start + k] = split(ext[start + k])

    def split_tiles(low, high):
        @pl.loop(low, high)
        def _(chunk):
            load(chunk).wait()
            at = lax.rem(chunk, 2)

            @pl.loop(0, UNIT)
            def _(k):
                tile_parts[chunk * UNIT + k] = split(stage[at, k])

            @pl.when(chunk + 2 < n_own // UNIT)
            def _():
                load(chunk + 2).start()

    def rim_copy(piece):
        up = piece < 2
        src = total - 2 * RIM + piece * UNIT if up else RIM + (piece - 2) * UNIT
        dst = piece * UNIT if up else total - RIM + (piece - 2) * UNIT
        peer = lax.rem(g + 1, groups) if up else lax.rem(g + groups - 1, groups)
        return pltpu.make_async_remote_copy(
            src_ref=ext.at[pl.ds(src, UNIT)], dst_ref=ext.at[pl.ds(dst, UNIT)],
            send_sem=rim_send.at[piece], recv_sem=rim_recv.at[piece],
            device_id={"grp": peer}, device_id_type=MESH,
        )

    def rim_leaves(origin, sub):
        at = place(origin)
        sends = (at == last) & (g < groups - 1) if sub >= 2 else (at == 0) & (g > 0)

        @pl.when(sends)
        def _():
            rim_copy(sub - 2 if sub >= 2 else sub + 2).start()

    def base_of(origin, sub):
        return RIM + place(origin) * blocks + sub * UNIT

    def quarter(origin, sub):
        return ext.at[pl.ds(base_of(origin, sub), UNIT)]

    here = set()
    fresh = []

    def need(origin, sub):
        name = unit_id(origin, sub)
        if name in here:
            return
        here.add(name)
        fresh.append((origin, sub))
        if name >= 4:
            link.arrive(quarter(origin, sub), name, neighbour(0, 1))

    def tidy():
        for origin, sub in fresh:
            rim_leaves(origin, sub)
        for origin, sub in fresh:
            split_unit(base_of(origin, sub))
        fresh.clear()

    base = 64

    def note_row(dx):
        return metas.at[lax.rem(x + dx + SIDE, SIDE) * SIDE + z]

    def note_wait(ref, arrival):
        link.arrive(ref, arrival, neighbour(0, 1))

    queues = gather_queues()
    turns = len(queues[0][2])
    chunks = n_own // UNIT
    for turn in range(turns):
        for axis, way, queue in queues:
            origin, sub = queue[turn]
            need(origin, sub)
            seen = (origin[0] - step(axis, way)[0], origin[1] - step(axis, way)[1])
            link.start(
                quarter(origin, sub), quarter(origin, sub), unit_id(seen, sub), neighbour(axis, way)
            )
        if turn == 0:
            link.start(note_row(0), note_row(0), base, neighbour(0, 1))
            link.start(note_row(0), note_row(0), base + 1, neighbour(0, -1))
        if turn == 3:
            note_wait(note_row(-1), base)
            note_wait(note_row(1), base + 1)
            link.start(note_row(-1), note_row(-1), base + 2, neighbour(0, 1))
        if turn == 6:
            note_wait(note_row(2), base + 2)
            for dx in range(SIDE):
                link.start(note_row(dx), note_row(dx), base + 3 + dx, neighbour(1, 1))
                link.start(note_row(dx), note_row(dx), base + 7 + dx, neighbour(1, -1))
        if turn == 9:
            for dx in range(SIDE):
                behind = metas.at[place((dx, -1))]
                note_wait(behind, base + 3 + dx)
                note_wait(metas.at[place((dx, 1))], base + 7 + dx)
                link.start(behind, behind, base + 11 + dx, neighbour(1, 1))
        tidy()
        if turn == 1:
            for copy in vectors:
                copy.wait()
            order_table(vec[0], vec[1], table)
            fetch(table, order, 6).wait()
        split_tiles(chunks * turn // turns, chunks * (turn + 1) // turns)
    of_ext = len(link.sent)
    for dx in range(SIDE):
        note_wait(metas.at[place((dx, 2))], base + 11 + dx)
    base += 15
    for bundle in bundles:
        bundle.wait()

    def bundle_of(slot, to):
        at = place(to)
        return helps.at[at // SIDE, :, 0] if slot == 0 else helps.at[:, lax.rem(at, SIDE), 1]

    def pair_of(slot, to, low):
        at = place(to)
        part = pl.ds(low, 2)
        return helps.at[at // SIDE, part, 0] if slot == 0 else helps.at[part, lax.rem(at, SIDE), 1]

    def final(slot, along, across):
        return arrived.at[slot, along % SIDE, across % SIDE - 1]

    def arrival(slot, kind):
        return base + slot * 28 + kind

    def target(slot, way):
        axis = 1 - slot
        at = place(step(axis, way))
        return lax.rem(at, SIDE) if axis == 1 else at // SIDE

    def opening(slot):
        for way, low in ((1, 0), (-1, 2)):
            k = 0 if way > 0 else 1
            link.start(
                pair_of(slot, step(slot, 2), low), passing.at[slot, k], arrival(slot, k),
                neighbour(slot, way),
            )
            link.start(
                bundle_of(slot, step(slot, way)), first.at[slot, -way % SIDE],
                arrival(slot, 2 + k), neighbour(slot, way),
            )

    def relay(slot):
        for way, low in ((1, 0), (-1, 2)):
            k = 0 if way > 0 else 1
            note_wait(passing.at[slot, k], arrival(slot, k))
            link.start(
                passing.at[slot, k], first.at[slot, 2, pl.ds(low, 2)], arrival(slot, 4 + k),
                neighbour(slot, way),
            )

    def direct(slot, along):
        for way in (1, -1):
            link.start(
                first.at[slot, along % SIDE, target(slot, way)], final(slot, along, -way),
                arrival(slot, 6 + (along % SIDE) * 4 + (-way) % SIDE), neighbour(1 - slot, way),
            )

    by = {0: 1, 1: 1, 3: -1, 2: -1}

    def detour(slot, along):
        way = by[along % SIDE]
        link.start(
            first.at[slot, along % SIDE, target(slot, 2)], second.at[slot, along % SIDE],
            arrival(slot, 22 + along % SIDE), neighbour(1 - slot, way),
        )

    def hand_on(slot, along):
        way = by[along % SIDE]
        note_wait(second.at[slot, along % SIDE], arrival(slot, 22 + along % SIDE))
        link.start(
            second.at[slot, along % SIDE], final(slot, along, 2),
            arrival(slot, 6 + (along % SIDE) * 4 + 2), neighbour(1 - slot, way),
        )

    def bundle_wait(slot, way):
        k = 0 if way > 0 else 1
        note_wait(first.at[slot, -way % SIDE], arrival(slot, 2 + k))

    slots = (0, 1)
    for slot in slots:
        opening(slot)
    for slot in slots:
        detour(slot, 0)
        direct(slot, 0)
    scalars = fetch(metas, notes, 1)
    notes_copy = fetch(metas, notes_out, 2)

    for a in range(SIDE):
        for b in range(SIDE):
            for sub in range(4):
                need((a, b), sub)
    tidy()

    def rim(has, pieces, start):
        @pl.when(has)
        def _():
            for piece in pieces:
                rim_copy(piece).wait_recv()
            for k in range(RIM // UNIT):
                split_unit(start + k * UNIT)

        @pl.when(jnp.logical_not(has))
        def _():
            ext_parts[start : start + RIM] = jnp.zeros((RIM,) + ext_parts.shape[1:], jnp.bfloat16)

    rim(g > 0, (0, 1), 0)
    rim(g < groups - 1, (2, 3), total - RIM)
    for copy in link.sent[:of_ext]:
        copy.wait_send()

    @pl.when(g < groups - 1)
    def _():
        for piece in (0, 1):
            rim_copy(piece).wait_send()

    @pl.when(g > 0)
    def _():
        for piece in (2, 3):
            rim_copy(piece).wait_send()

    def own(low, high):
        def body(k, acc):
            for u in range(UNROLL):
                at = low + k * UNROLL + u
                keep = order[2, at].astype(jnp.float32)
                acc = acc * keep + product(tile_parts[order[0, at]], ext_parts[order[1, at]])
                ext[at] = acc
            return acc

        acc = jnp.zeros(ext.shape[1:], jnp.float32) if low == 0 else ext[low - 1]
        lax.fori_loop(0, (high - low) // UNROLL, body, acc)

    def help_product(k, slot):
        along, across = HELP_ORDER[k]
        if across == 0:
            tile = first[slot, along, target(slot, 0)]
        else:
            note_wait(final(slot, along, across), arrival(slot, 6 + along * 4 + across))
            tile = arrived[slot, along, across - 1]
        source = place((along, across) if slot == 0 else (across, along))
        col = notes[source, 0, 0, n * 2 + slot]
        terms[k * 2 + slot] = product(split(tile), ext_parts[col])

    def help_products(low, high):
        for k in range(low, high):
            for slot in slots:
                help_product(k, slot)

    quart = n_own // 4
    own(0, quart)
    for slot in slots:
        relay(slot)
    own(quart, 2 * quart)
    for slot in slots:
        for way in (1, -1):
            bundle_wait(slot, way)
    for slot in slots:
        direct(slot, -1)
        direct(slot, 1)
        detour(slot, 1)
        detour(slot, -1)
    own(2 * quart, 3 * quart)
    for slot in slots:
        hand_on(slot, 0)
    own(3 * quart, n_own)

    @pl.loop(0, blocks)
    def _(row):
        sums[row] = ext[order[3, row]] * order[4, row].astype(jnp.float32)

    sums_copy = fetch(sums, sums_out, 3)
    scalars.wait()
    for slot in slots:
        for k, low in ((0, 0), (1, 2)):
            note_wait(first.at[slot, 2, pl.ds(low, 2)], arrival(slot, 4 + k))
        detour(slot, 2)
        direct(slot, 2)
    help_products(0, 3)
    for slot in slots:
        hand_on(slot, 1)
        hand_on(slot, -1)
    help_products(3, 8)
    for slot in slots:
        hand_on(slot, 2)
    help_products(8, 13)
    early = 26
    terms_copy = fetch(terms.at[pl.ds(0, early)], terms_out.at[pl.ds(0, early)], 4)
    help_products(13, 16)
    rest = terms.shape[0] - early
    rest_copy = fetch(terms.at[pl.ds(early, rest)], terms_out.at[pl.ds(early, rest)], 5)
    for copy in link.sent[of_ext:]:
        copy.wait_send()
    for copy in (notes_copy, sums_copy, terms_copy, rest_copy):
        copy.wait()


def add_terms(notes_in, sums, terms_in, total, terms, notes, sem):
    copies = [
        pltpu.make_async_copy(notes_in, notes, sem.at[0]),
        pltpu.make_async_copy(sums, total, sem.at[1]),
        pltpu.make_async_copy(terms_in, terms, sem.at[2]),
    ]
    for copy in copies:
        copy.start()
    n = lax.axis_index("nbr")
    x, z = n // SIDE, lax.rem(n, SIDE)
    for copy in copies:
        copy.wait()
    for k, (along, across) in enumerate(HELP_ORDER):
        for slot in (0, 1):
            dx, dz = (along, across) if slot == 0 else (across, along)
            source = lax.rem(x + dx, SIDE) * SIDE + lax.rem(z + dz, SIDE)
            at = n * 2 + slot
            row, live = notes[source, 1, 0, at], notes[source, 2, 0, at]
            total[row] += terms[k * 2 + slot] * live.astype(jnp.float32)


def local(sims, own_tiles, own_cols, own_rows, help_tiles, help_cols, help_rows, help_live):
    blocks, size = sims.shape[0], sims.shape[1:]
    neighbours = lax.axis_size("nbr")
    helps, owns = help_tiles.shape[0], own_tiles.shape[0]
    extended = blocks * neighbours + 2 * RIM
    parts = (size[0], 2 * size[1])
    any_space = pl.BlockSpec(memory_space=pl.ANY)
    f32, bf16, i32 = jnp.float32, jnp.bfloat16, jnp.int32
    sums, terms, notes = pl.pallas_call(
        exchange,
        out_shape=(
            jax.ShapeDtypeStruct(sims.shape, f32),
            jax.ShapeDtypeStruct(help_tiles.shape, f32),
            jax.ShapeDtypeStruct((neighbours, 3, 1, helps), i32),
        ),
        in_specs=[any_space] * 8,
        out_specs=(any_space,) * 3,
        scratch_shapes=[
            pltpu.VMEM((extended,) + size, f32),
            pltpu.VMEM((extended,) + parts, bf16),
            pltpu.VMEM((owns,) + parts, bf16),
            pltpu.VMEM((2, UNIT) + size, f32),
            pltpu.VMEM((2, SIDE, SIDE) + size, f32),
            pltpu.VMEM((2, 2, 2) + size, f32),
            pltpu.VMEM((2, SIDE) + size, f32),
            pltpu.VMEM((2, SIDE, SIDE - 1) + size, f32),
            pltpu.VMEM((helps,) + size, f32),
            pltpu.VMEM(sims.shape, f32),
            pltpu.VMEM((neighbours, 3, 1, helps), i32),
            pltpu.VMEM((2, 1, owns), i32),
            pltpu.VMEM((8, 256), i32),
            pltpu.SMEM((8, 256), i32),
            pltpu.SMEM((neighbours, 3, 1, helps), i32),
            pltpu.SemaphoreType.DMA((160,)),
            pltpu.SemaphoreType.DMA((160,)),
            pltpu.SemaphoreType.DMA((4,)),
            pltpu.SemaphoreType.DMA((4,)),
            pltpu.SemaphoreType.DMA((8,)),
            pltpu.SemaphoreType.DMA((2,)),
        ],
        compiler_params=pltpu.CompilerParams(
            collective_id=0, has_side_effects=True, vmem_limit_bytes=63 * 2**20
        ),
        name="exchange",
    )(
        sims,
        help_tiles.reshape((SIDE, SIDE, 2) + size),
        own_tiles,
        *(v.reshape(1, -1) for v in (own_cols, own_rows, help_cols, help_rows, help_live)),
    )
    return pl.pallas_call(
        add_terms,
        out_shape=jax.ShapeDtypeStruct(sims.shape, f32),
        in_specs=[any_space] * 3,
        out_specs=pl.BlockSpec(memory_space=pltpu.VMEM),
        scratch_shapes=[
            pltpu.VMEM(help_tiles.shape, f32),
            pltpu.SMEM((neighbours, 3, 1, helps), i32),
            pltpu.SemaphoreType.DMA((3,)),
        ],
        name="add_terms",
    )(notes, sums, terms)


def solution(mesh):
    whole, flat = P(("grp", "nbr"), None, None), P(("grp", "nbr"))
    placed = (whole, whole, flat, flat, whole, flat, flat, flat)
    return jax.shard_map(local, mesh=mesh, in_specs=placed, out_specs=whole, check_vma=False)
```

```python
import jax
import jax.numpy as jnp
from jax import lax
from jax.experimental import pallas as pl
from jax.experimental.pallas import tpu as pltpu
from jax.sharding import PartitionSpec as P

RIM = 8
UNIT = 4
SIDE = 4
UNROLL = 16
MESH = pl.DeviceIdType.MESH


def wrap(value):
    return (value + SIDE) % SIDE if isinstance(value, int) else lax.rem(value + SIDE, SIDE)


def unit_id(origin, sub):
    return (wrap(origin[0]) * SIDE + wrap(origin[1])) * 4 + sub


def gather_queues():
    queues = []
    for axis in (0, 1):
        for way in (1, -1):
            near, far = ((0, 1), (2, 3)) if axis == 0 else ((2, 3), (0, 1))
            if way < 0:
                near, far = near[::-1], far[::-1]

            def at(along, across, axis=axis):
                return (along, across) if axis == 0 else (across, along)

            queue = [
                (at(0, 0), near[0]),
                (at(0, 0), near[1]),
                (at(0, 0), far[0]),
                (at(-way, 0), near[0]),
                (at(0, 0), far[1]),
                (at(0, -1), far[0]),
                (at(0, 1), far[0]),
                (at(0, -1), far[1]),
                (at(0, 1), far[1]),
                (at(0, 2), far[0]),
                (at(0, 2), far[1]),
            ]
            queues.append((axis, way, queue, far[0]))
    return queues


class Link:
    def __init__(self, send, recv):
        self.send, self.recv, self.sent = send, recv, []

    def start(self, src, dst, arrival, device):
        copy = pltpu.make_async_remote_copy(
            src_ref=src,
            dst_ref=dst,
            send_sem=self.send.at[len(self.sent)],
            recv_sem=self.recv.at[arrival],
            device_id=device,
            device_id_type=MESH,
        )
        copy.start()
        self.sent.append(copy)

    def arrive(self, dst, arrival, device):
        pltpu.make_async_remote_copy(
            src_ref=dst,
            dst_ref=dst,
            send_sem=self.send.at[0],
            recv_sem=self.recv.at[arrival],
            device_id=device,
            device_id_type=MESH,
        ).wait_recv()


def split(value):
    high = value.astype(jnp.bfloat16)
    low = (value - high.astype(jnp.float32)).astype(jnp.bfloat16)
    return jnp.concatenate([high, low], axis=1)


def product(tile, block):
    both = jnp.dot(
        tile, jnp.concatenate([block, block], axis=0), preferred_element_type=jnp.float32
    )
    half = both.shape[1] // 2
    return both[:, :half] + both[:, half:]


def order_table(cols, rows, table):
    count = rows.shape[1]
    table[...] = jnp.zeros_like(table)
    line = lax.broadcasted_iota(jnp.int32, (count, count), 1)
    deep = lax.broadcasted_iota(jnp.int32, (count, count), 0)

    def upright(value):
        return jnp.sum(jnp.where(line == deep, value, 0), axis=1, keepdims=True)

    key = rows * 256 + line[:1]
    key_up, col_up = upright(key), upright(cols)
    row_up = jnp.right_shift(key_up, 8)
    rank = jnp.sum((key < key_up).astype(jnp.int32), axis=1, keepdims=True)
    here = rank == line
    before = rank == line - 1
    row_at = jnp.sum(jnp.where(here, row_up, 0), axis=0, keepdims=True)
    row_before = jnp.sum(jnp.where(before, row_up + 1, 0), axis=0, keepdims=True) - 1
    table[0:1, :count] = jnp.sum(jnp.where(here, deep, 0), axis=0, keepdims=True)
    table[1:2, :count] = jnp.sum(jnp.where(here, col_up, 0), axis=0, keepdims=True)
    table[2:3, :count] = (row_at == row_before).astype(jnp.int32)
    upto = jnp.sum((row_up <= line).astype(jnp.int32), axis=0, keepdims=True)
    table[3:4, :count] = jnp.maximum(upto - 1, 0)
    table[4:5, :count] = jnp.minimum(
        jnp.sum((row_up == line).astype(jnp.int32), axis=0, keepdims=True), 1
    )


HELP_ORDER = (
    [(0, 0), (1, 0), (3, 0), (2, 0), (0, 1), (0, 3), (1, 1), (1, 3)]
    + [(3, 1), (3, 3), (2, 1), (2, 3), (0, 2), (3, 2), (1, 2), (2, 2)]
)
LATE = 2


def exchange(
    sims, helps, tiles, own_cols, own_rows, help_cols, help_rows, help_live,
    sums_out,
    ext, ext_parts, tile_parts, stage, first, passing, second, arrived, terms, sums,
    metas, vec, table, order, help_order, notes,
    send, recv, rim_send, rim_recv, local_sem, stage_sem,
):
    n, g = lax.axis_index("nbr"), lax.axis_index("grp")
    groups = lax.axis_size("grp")
    x, z = n // SIDE, lax.rem(n, SIDE)
    blocks = sims.shape[0]
    total = ext.shape[0]
    n_own = tiles.shape[0]
    last = SIDE * SIDE - 1

    def place(origin):
        return lax.rem(x + origin[0] + SIDE, SIDE) * SIDE + lax.rem(z + origin[1] + SIDE, SIDE)

    def step(axis, way):
        return (way, 0) if axis == 0 else (0, way)

    def neighbour(axis, way):
        return {"nbr": place(step(axis, way))}

    barrier = pltpu.get_barrier_semaphore()
    for axis in (0, 1):
        for way in (1, -1):
            pl.semaphore_signal(barrier, inc=1, device_id=neighbour(axis, way), device_id_type=MESH)

    @pl.when(g > 0)
    def _():
        pl.semaphore_signal(barrier, inc=1, device_id={"grp": g - 1}, device_id_type=MESH)

    @pl.when(g < groups - 1)
    def _():
        pl.semaphore_signal(barrier, inc=1, device_id={"grp": g + 1}, device_id_type=MESH)

    def fetch(src, dst, k):
        copy = pltpu.make_async_copy(src, dst, local_sem.at[k])
        copy.start()
        return copy

    mine = fetch(sims, ext.at[pl.ds(RIM + n * blocks, blocks)], 0)
    told = [
        fetch(ref, metas.at[n, k], 1 + k) for k, ref in enumerate((help_cols, help_rows, help_live))
    ]
    bundles = [
        fetch(helps.at[x, :, 0], first.at[0, 0], 4), fetch(helps.at[:, z, 1], first.at[1, 0], 5)
    ]
    vectors = [fetch(own_cols, vec.at[0], 6), fetch(own_rows, vec.at[1], 7)]

    def load(chunk):
        at = lax.rem(chunk, 2)
        return pltpu.make_async_copy(
            tiles.at[pl.ds(chunk * UNIT, UNIT)], stage.at[at], stage_sem.at[at]
        )

    for chunk in (0, 1):
        load(chunk).start()

    pl.semaphore_wait(
        barrier, 4 + (g > 0).astype(jnp.int32) + (g < groups - 1).astype(jnp.int32)
    )
    mine.wait()
    for copy in told:
        copy.wait()
    link = Link(send, recv)

    def split_unit(start):
        @pl.loop(0, UNIT)
        def _(k):
            ext_parts[start + k] = split(ext[start + k])

    def split_tiles(low, high):
        @pl.loop(low, high)
        def _(chunk):
            load(chunk).wait()
            at = lax.rem(chunk, 2)

            @pl.loop(0, UNIT)
            def _(k):
                tile_parts[chunk * UNIT + k] = split(stage[at, k])

            @pl.when(chunk + 2 < n_own // UNIT)
            def _():
                load(chunk + 2).start()

    def rim_copy(piece):
        up = piece < 2
        src = total - 2 * RIM + piece * UNIT if up else RIM + (piece - 2) * UNIT
        dst = piece * UNIT if up else total - RIM + (piece - 2) * UNIT
        peer = lax.rem(g + 1, groups) if up else lax.rem(g + groups - 1, groups)
        return pltpu.make_async_remote_copy(
            src_ref=ext.at[pl.ds(src, UNIT)], dst_ref=ext.at[pl.ds(dst, UNIT)],
            send_sem=rim_send.at[piece], recv_sem=rim_recv.at[piece],
            device_id={"grp": peer}, device_id_type=MESH,
        )

    def rim_leaves(origin, sub):
        at = place(origin)
        sends = (at == last) & (g < groups - 1) if sub >= 2 else (at == 0) & (g > 0)

        @pl.when(sends)
        def _():
            rim_copy(sub - 2 if sub >= 2 else sub + 2).start()

    def base_of(origin, sub):
        return RIM + place(origin) * blocks + sub * UNIT

    def quarter(origin, sub):
        return ext.at[pl.ds(base_of(origin, sub), UNIT)]

    here = set()
    fresh = []

    def need(origin, sub):
        name = unit_id(origin, sub)
        if name in here:
            return
        here.add(name)
        fresh.append((origin, sub))
        if name >= 4:
            link.arrive(quarter(origin, sub), name, neighbour(0, 1))

    def tidy():
        for origin, sub in fresh:
            rim_leaves(origin, sub)
        for origin, sub in fresh:
            split_unit(base_of(origin, sub))
        fresh.clear()

    base = 64

    def note_row(dx):
        return metas.at[lax.rem(x + dx + SIDE, SIDE) * SIDE + z]

    def note_wait(ref, arrival):
        link.arrive(ref, arrival, neighbour(0, 1))

    def bundle_of(slot, to):
        at = place(to)
        return helps.at[at // SIDE, :, 0] if slot == 0 else helps.at[:, lax.rem(at, SIDE), 1]

    def pair_of(slot, to, low):
        at = place(to)
        part = pl.ds(low, 2)
        return helps.at[at // SIDE, part, 0] if slot == 0 else helps.at[part, lax.rem(at, SIDE), 1]

    def final(slot, along, across):
        return arrived.at[slot, along % SIDE, across % SIDE - 1]

    def arrival(slot, kind):
        return 79 + slot * 28 + kind

    def target(slot, way):
        axis = 1 - slot
        at = place(step(axis, way))
        return lax.rem(at, SIDE) if axis == 1 else at // SIDE

    def far_pairs(slot):
        for way, low in ((1, 0), (-1, 2)):
            k = 0 if way > 0 else 1
            link.start(
                pair_of(slot, step(slot, 2), low), passing.at[slot, k], arrival(slot, k),
                neighbour(slot, way),
            )

    def bundle(slot):
        for way in (1, -1):
            link.start(
                bundle_of(slot, step(slot, way)), first.at[slot, -way % SIDE],
                arrival(slot, 2 + (0 if way > 0 else 1)), neighbour(slot, way),
            )

    def relay(slot):
        for way, low in ((1, 0), (-1, 2)):
            k = 0 if way > 0 else 1
            note_wait(passing.at[slot, k], arrival(slot, k))
            link.start(
                passing.at[slot, k], first.at[slot, 2, pl.ds(low, 2)], arrival(slot, 4 + k),
                neighbour(slot, way),
            )

    def direct(slot, along):
        for way in (1, -1):
            link.start(
                first.at[slot, along % SIDE, target(slot, way)], final(slot, along, -way),
                arrival(slot, 6 + (along % SIDE) * 4 + (-way) % SIDE), neighbour(1 - slot, way),
            )

    by = {0: 1, 1: 1, 3: -1, 2: -1}

    def detour(slot, along):
        way = by[along % SIDE]
        link.start(
            first.at[slot, along % SIDE, target(slot, 2)], second.at[slot, along % SIDE],
            arrival(slot, 22 + along % SIDE), neighbour(1 - slot, way),
        )

    def hand_on(slot, along):
        way = by[along % SIDE]
        note_wait(second.at[slot, along % SIDE], arrival(slot, 22 + along % SIDE))
        link.start(
            second.at[slot, along % SIDE], final(slot, along, 2),
            arrival(slot, 6 + (along % SIDE) * 4 + 2), neighbour(1 - slot, way),
        )

    def bundle_wait(slot, way):
        k = 0 if way > 0 else 1
        note_wait(first.at[slot, -way % SIDE], arrival(slot, 2 + k))

    slots = (0, 1)

    def rim(has, pieces, start):
        @pl.when(has)
        def _():
            for piece in pieces:
                rim_copy(piece).wait_recv()
            for k in range(RIM // UNIT):
                split_unit(start + k * UNIT)

        @pl.when(jnp.logical_not(has))
        def _():
            ext_parts[start : start + RIM] = jnp.zeros((RIM,) + ext_parts.shape[1:], jnp.bfloat16)

    def noted(k, slot):
        along, across = HELP_ORDER[k]
        source = place((along, across) if slot == 0 else (across, along))
        return [notes[source, kind, 0, n * 2 + slot] for kind in range(3)]

    def list_rows():
        spots = lax.broadcasted_iota(jnp.int32, (1, terms.shape[0]), 1)
        help_rows_line = jnp.full_like(spots, blocks)
        help_live_line = jnp.zeros_like(spots)
        for k in range(len(HELP_ORDER) - LATE):
            for slot in slots:
                _, row, live = noted(k, slot)
                help_rows_line = jnp.where(spots == k * 2 + slot, row, help_rows_line)
                help_live_line = jnp.where(spots == k * 2 + slot, live, help_live_line)
        order_table(help_live_line, help_rows_line, table)
        help_table = fetch(table, help_order, 2)
        return help_table

    queues = gather_queues()
    turns = len(queues[0][2])
    chunks = n_own // UNIT
    for turn in range(turns):
        for axis, way, queue, _ in queues:
            origin, sub = queue[turn]
            need(origin, sub)
            seen = (origin[0] - step(axis, way)[0], origin[1] - step(axis, way)[1])
            link.start(
                quarter(origin, sub), quarter(origin, sub), unit_id(seen, sub), neighbour(axis, way)
            )
        if turn == 0:
            link.start(note_row(0), note_row(0), base, neighbour(0, 1))
            link.start(note_row(0), note_row(0), base + 1, neighbour(0, -1))
        if turn == 3:
            note_wait(note_row(-1), base)
            note_wait(note_row(1), base + 1)
            link.start(note_row(-1), note_row(-1), base + 2, neighbour(0, 1))
        if turn == 6:
            note_wait(note_row(2), base + 2)
            for dx in range(SIDE):
                link.start(note_row(dx), note_row(dx), base + 3 + dx, neighbour(1, 1))
                link.start(note_row(dx), note_row(dx), base + 7 + dx, neighbour(1, -1))
        if turn == 9:
            for dx in range(SIDE):
                behind = metas.at[place((dx, -1))]
                note_wait(behind, base + 3 + dx)
                note_wait(metas.at[place((dx, 1))], base + 7 + dx)
                link.start(behind, behind, base + 11 + dx, neighbour(1, 1))
        for slot in slots:
            if turn == 5:
                far_pairs(slot)
            if turn == 8:
                relay(slot)
            if turn == turns - 1:
                bundle(slot)
        tidy()
        if turn == 1:
            for copy in vectors:
                copy.wait()
            order_table(vec[0], vec[1], table)
            fetch(table, order, 6).wait()
        split_tiles(chunks * turn // turns, chunks * (turn + 1) // turns)

    for axis, way, _, sub in queues:
        for across in range(SIDE):
            need((-way, across) if axis == 0 else (across, -way), sub)

    def ahead(axis, k):
        lead = SIDE - 1 - z if axis == 0 else SIDE - x
        return lax.rem(lead + k, SIDE)

    for k in range(SIDE):
        for axis, way, _, sub in queues:
            across = ahead(axis, k)
            origin = (-way, across) if axis == 0 else (across, -way)
            seen = (-2, across) if axis == 0 else (across, -2)
            link.start(
                quarter(origin, sub), quarter(origin, sub), unit_id(seen, sub), neighbour(axis, way)
            )
    of_ext = len(link.sent)
    for a in range(SIDE):
        for b in range(SIDE):
            for sub in range(4):
                if not (a == 2 and sub >= 2 or b == 2 and sub < 2):
                    need((a, b), sub)
    tidy()
    for copy in bundles:
        copy.wait()

    for slot in slots:
        for k, low in ((0, 0), (1, 2)):
            note_wait(first.at[slot, 2, pl.ds(low, 2)], arrival(slot, 4 + k))
        for way in (1, -1):
            bundle_wait(slot, way)
    for along in (0, 3, 1, 2):
        for slot in slots:
            detour(slot, along)
    for along in (0, 1, 3, 2):
        for slot in slots:
            direct(slot, along)
    for dx in range(SIDE):
        note_wait(metas.at[place((dx, 2))], base + 11 + dx)
    fetch(metas, notes, 1).wait()

    for k in range(SIDE):
        for axis, way, _, sub in queues:
            across = ahead(axis, k)
            origin = (2, across) if axis == 0 else (across, 2)
            link.arrive(quarter(origin, sub), unit_id(origin, sub), neighbour(0, 1))
            fresh.append((origin, sub))
        tidy()
        if k == 0:
            help_table = list_rows()
    rim(g > 0, (0, 1), 0)
    rim(g < groups - 1, (2, 3), total - RIM)
    for copy in link.sent[:of_ext]:
        copy.wait_send()

    @pl.when(g < groups - 1)
    def _():
        for piece in (0, 1):
            rim_copy(piece).wait_send()

    @pl.when(g > 0)
    def _():
        for piece in (2, 3):
            rim_copy(piece).wait_send()

    def own(low, high):
        def body(k, acc):
            for u in range(UNROLL):
                at = low + k * UNROLL + u
                keep = order[2, at].astype(jnp.float32)
                acc = acc * keep + product(tile_parts[order[0, at]], ext_parts[order[1, at]])
                ext[at] = acc
            return acc

        acc = jnp.zeros(ext.shape[1:], jnp.float32) if low == 0 else ext[low - 1]
        lax.fori_loop(0, (high - low) // UNROLL, body, acc)

    def help_products(low, high):
        for k in range(low, high):
            along, across = HELP_ORDER[k]
            for slot in slots:
                if across:
                    note_wait(final(slot, along, across), arrival(slot, 6 + along * 4 + across))
        for k in range(low, high):
            along, across = HELP_ORDER[k]
            for slot in slots:
                tile = (
                    arrived[slot, along, across - 1]
                    if across
                    else first[slot, along, target(slot, 0)]
                )
                terms[k * 2 + slot] = product(split(tile), ext_parts[noted(k, slot)[0]])

    cut = n_own // 2
    own(0, cut)
    for along in (0, 3, 1, 2):
        for slot in slots:
            hand_on(slot, along)
    own(cut, n_own)

    @pl.loop(0, blocks)
    def _(row):
        sums[row] = ext[order[3, row]] * order[4, row].astype(jnp.float32)

    help_products(0, 4)
    help_products(4, 8)
    help_products(8, 12)
    help_products(12, 14)
    help_table.wait()
    acc = jnp.zeros(ext.shape[1:], jnp.float32)
    for at in range(2 * (len(HELP_ORDER) - LATE)):
        keep = help_order[2, at].astype(jnp.float32)
        live = help_order[1, at].astype(jnp.float32)
        acc = acc * keep + terms[help_order[0, at]] * live
        ext[at] = acc

    @pl.loop(0, blocks)
    def _(row):
        sums[row] += ext[help_order[3, row]] * help_order[4, row].astype(jnp.float32)

    help_products(14, 16)

    @pl.loop(0, blocks)
    def _(row):
        acc = sums[row]
        for k in range(len(HELP_ORDER) - LATE, len(HELP_ORDER)):
            for slot in slots:
                _, at, live = noted(k, slot)
                share = (at == row).astype(jnp.float32) * live.astype(jnp.float32)
                acc += terms[k * 2 + slot] * share
        sums_out[row] = acc

    for copy in link.sent[of_ext:]:
        copy.wait_send()


def local(sims, own_tiles, own_cols, own_rows, help_tiles, help_cols, help_rows, help_live):
    blocks, size = sims.shape[0], sims.shape[1:]
    neighbours = lax.axis_size("nbr")
    helps, owns = help_tiles.shape[0], own_tiles.shape[0]
    extended = blocks * neighbours + 2 * RIM
    parts = (size[0], 2 * size[1])
    any_space = pl.BlockSpec(memory_space=pl.ANY)
    f32, bf16, i32 = jnp.float32, jnp.bfloat16, jnp.int32
    return pl.pallas_call(
        exchange,
        out_shape=pltpu.VMEM(sims.shape, f32),
        in_specs=[any_space] * 8,
        out_specs=pl.BlockSpec(memory_space=pltpu.VMEM),
        scratch_shapes=[
            pltpu.VMEM((extended,) + size, f32),
            pltpu.VMEM((extended,) + parts, bf16),
            pltpu.VMEM((owns,) + parts, bf16),
            pltpu.VMEM((2, UNIT) + size, f32),
            pltpu.VMEM((2, SIDE, SIDE) + size, f32),
            pltpu.VMEM((2, 2, 2) + size, f32),
            pltpu.VMEM((2, SIDE) + size, f32),
            pltpu.VMEM((2, SIDE, SIDE - 1) + size, f32),
            pltpu.VMEM((helps,) + size, f32),
            pltpu.VMEM(sims.shape, f32),
            pltpu.VMEM((neighbours, 3, 1, helps), i32),
            pltpu.VMEM((2, 1, owns), i32),
            pltpu.VMEM((8, 256), i32),
            pltpu.SMEM((8, 256), i32),
            pltpu.SMEM((8, 256), i32),
            pltpu.SMEM((neighbours, 3, 1, helps), i32),
            pltpu.SemaphoreType.DMA((160,)),
            pltpu.SemaphoreType.DMA((160,)),
            pltpu.SemaphoreType.DMA((4,)),
            pltpu.SemaphoreType.DMA((4,)),
            pltpu.SemaphoreType.DMA((8,)),
            pltpu.SemaphoreType.DMA((2,)),
        ],
        compiler_params=pltpu.CompilerParams(
            collective_id=0, has_side_effects=True, vmem_limit_bytes=57 * 2**20
        ),
        name="exchange",
    )(
        sims,
        help_tiles.reshape((SIDE, SIDE, 2) + size),
        own_tiles,
        *(v.reshape(1, -1) for v in (own_cols, own_rows, help_cols, help_rows, help_live)),
    )


def solution(mesh):
    whole, flat = P(("grp", "nbr"), None, None), P(("grp", "nbr"))
    placed = (whole, whole, flat, flat, whole, flat, flat, flat)
    return jax.shard_map(local, mesh=mesh, in_specs=placed, out_specs=whole, check_vma=False)
```

```python
import jax
import jax.numpy as jnp
from jax import lax
from jax.experimental import pallas as pl
from jax.experimental.pallas import tpu as pltpu
from jax.sharding import PartitionSpec as P

RIM = 8
UNIT = 4
SIDE = 4
UNROLL = 16
MESH = pl.DeviceIdType.MESH


def wrap(value):
    return (value + SIDE) % SIDE if isinstance(value, int) else lax.rem(value + SIDE, SIDE)


def unit_id(origin, sub):
    return (wrap(origin[0]) * SIDE + wrap(origin[1])) * 4 + sub


def gather_queues():
    queues = []
    for axis in (0, 1):
        for way in (1, -1):
            near, far = ((0, 1), (2, 3)) if axis == 0 else ((2, 3), (0, 1))
            if way < 0:
                near, far = near[::-1], far[::-1]

            def at(along, across, axis=axis):
                return (along, across) if axis == 0 else (across, along)

            queue = [
                (at(0, 0), near[0]),
                (at(0, 0), near[1]),
                (at(0, 0), far[0]),
                (at(-way, 0), near[0]),
                (at(0, 0), far[1]),
                (at(0, -1), far[0]),
                (at(0, 1), far[0]),
                (at(0, -1), far[1]),
                (at(0, 1), far[1]),
                (at(0, 2), far[0]),
                (at(0, 2), far[1]),
            ]
            queues.append((axis, way, queue, far[0]))
    return queues


class Link:
    def __init__(self, send, recv):
        self.send, self.recv, self.sent = send, recv, []

    def start(self, src, dst, arrival, device):
        copy = pltpu.make_async_remote_copy(
            src_ref=src,
            dst_ref=dst,
            send_sem=self.send.at[len(self.sent)],
            recv_sem=self.recv.at[arrival],
            device_id=device,
            device_id_type=MESH,
        )
        copy.start()
        self.sent.append(copy)

    def arrive(self, dst, arrival, device):
        pltpu.make_async_remote_copy(
            src_ref=dst,
            dst_ref=dst,
            send_sem=self.send.at[0],
            recv_sem=self.recv.at[arrival],
            device_id=device,
            device_id_type=MESH,
        ).wait_recv()


def split(value):
    high = value.astype(jnp.bfloat16)
    low = (value - high.astype(jnp.float32)).astype(jnp.bfloat16)
    return jnp.concatenate([high, low], axis=1)


def product(tile, block):
    both = jnp.dot(
        tile, jnp.concatenate([block, block], axis=0), preferred_element_type=jnp.float32
    )
    half = both.shape[1] // 2
    return both[:, :half] + both[:, half:]


def order_table(cols, rows, table):
    count = rows.shape[1]
    table[...] = jnp.zeros_like(table)
    line = lax.broadcasted_iota(jnp.int32, (count, count), 1)
    deep = lax.broadcasted_iota(jnp.int32, (count, count), 0)

    def upright(value):
        return jnp.sum(jnp.where(line == deep, value, 0), axis=1, keepdims=True)

    key = rows * 256 + line[:1]
    key_up, col_up = upright(key), upright(cols)
    row_up = jnp.right_shift(key_up, 8)
    rank = jnp.sum((key < key_up).astype(jnp.int32), axis=1, keepdims=True)
    here = rank == line
    before = rank == line - 1
    row_at = jnp.sum(jnp.where(here, row_up, 0), axis=0, keepdims=True)
    row_before = jnp.sum(jnp.where(before, row_up + 1, 0), axis=0, keepdims=True) - 1
    table[0:1, :count] = jnp.sum(jnp.where(here, deep, 0), axis=0, keepdims=True)
    table[1:2, :count] = jnp.sum(jnp.where(here, col_up, 0), axis=0, keepdims=True)
    table[2:3, :count] = (row_at == row_before).astype(jnp.int32)
    upto = jnp.sum((row_up <= line).astype(jnp.int32), axis=0, keepdims=True)
    table[3:4, :count] = jnp.maximum(upto - 1, 0)
    table[4:5, :count] = jnp.minimum(
        jnp.sum((row_up == line).astype(jnp.int32), axis=0, keepdims=True), 1
    )


HELP_ORDER = (
    [(0, 0), (1, 0), (3, 0), (2, 0), (0, 1), (0, 3), (1, 1), (1, 3)]
    + [(3, 1), (3, 3), (2, 1), (2, 3), (0, 2), (3, 2), (1, 2), (2, 2)]
)
LATE = 2


def exchange(
    sims, helps, tiles, own_cols, own_rows, help_cols, help_rows, help_live,
    sums_out,
    ext, ext_parts, tile_parts, stage, first, passing, second, arrived, terms, sums,
    metas, vec, table, order, help_order, late_order, notes,
    send, recv, rim_send, rim_recv, local_sem, stage_sem,
):
    n, g = lax.axis_index("nbr"), lax.axis_index("grp")
    groups = lax.axis_size("grp")
    x, z = n // SIDE, lax.rem(n, SIDE)
    blocks = sims.shape[0]
    total = ext.shape[0]
    n_own = tiles.shape[0]
    last = SIDE * SIDE - 1

    def place(origin):
        return lax.rem(x + origin[0] + SIDE, SIDE) * SIDE + lax.rem(z + origin[1] + SIDE, SIDE)

    def step(axis, way):
        return (way, 0) if axis == 0 else (0, way)

    def neighbour(axis, way):
        return {"nbr": place(step(axis, way))}

    barrier = pltpu.get_barrier_semaphore()
    for axis in (0, 1):
        for way in (1, -1):
            pl.semaphore_signal(barrier, inc=1, device_id=neighbour(axis, way), device_id_type=MESH)

    @pl.when(g > 0)
    def _():
        pl.semaphore_signal(barrier, inc=1, device_id={"grp": g - 1}, device_id_type=MESH)

    @pl.when(g < groups - 1)
    def _():
        pl.semaphore_signal(barrier, inc=1, device_id={"grp": g + 1}, device_id_type=MESH)

    def fetch(src, dst, k):
        copy = pltpu.make_async_copy(src, dst, local_sem.at[k])
        copy.start()
        return copy

    def load(chunk):
        at = lax.rem(chunk, 2)
        return pltpu.make_async_copy(
            tiles.at[pl.ds(chunk * UNIT, UNIT)], stage.at[at], stage_sem.at[at]
        )

    pl.semaphore_wait(
        barrier, 4 + (g > 0).astype(jnp.int32) + (g < groups - 1).astype(jnp.int32)
    )
    link = Link(send, recv)

    def split_unit(start):
        @pl.loop(0, UNIT)
        def _(k):
            ext_parts[start + k] = split(ext[start + k])

    def split_tiles(low, high):
        @pl.loop(low, high)
        def _(chunk):
            load(chunk).wait()
            at = lax.rem(chunk, 2)

            @pl.loop(0, UNIT)
            def _(k):
                tile_parts[chunk * UNIT + k] = split(stage[at, k])

            @pl.when(chunk + 2 < n_own // UNIT)
            def _():
                load(chunk + 2).start()

    def rim_copy(piece):
        up = piece < 2
        src = total - 2 * RIM + piece * UNIT if up else RIM + (piece - 2) * UNIT
        dst = piece * UNIT if up else total - RIM + (piece - 2) * UNIT
        peer = lax.rem(g + 1, groups) if up else lax.rem(g + groups - 1, groups)
        return pltpu.make_async_remote_copy(
            src_ref=ext.at[pl.ds(src, UNIT)], dst_ref=ext.at[pl.ds(dst, UNIT)],
            send_sem=rim_send.at[piece], recv_sem=rim_recv.at[piece],
            device_id={"grp": peer}, device_id_type=MESH,
        )

    def rim_leaves(origin, sub):
        at = place(origin)
        sends = (at == last) & (g < groups - 1) if sub >= 2 else (at == 0) & (g > 0)

        @pl.when(sends)
        def _():
            rim_copy(sub - 2 if sub >= 2 else sub + 2).start()

    def base_of(origin, sub):
        return RIM + place(origin) * blocks + sub * UNIT

    def quarter(origin, sub):
        return ext.at[pl.ds(base_of(origin, sub), UNIT)]

    here = set()
    fresh = []

    def need(origin, sub):
        name = unit_id(origin, sub)
        if name in here:
            return
        here.add(name)
        fresh.append((origin, sub))
        if wrap(origin[0]) or wrap(origin[1]):
            link.arrive(quarter(origin, sub), name, neighbour(0, 1))

    def tidy():
        for origin, sub in fresh:
            rim_leaves(origin, sub)
        for origin, sub in fresh:
            split_unit(base_of(origin, sub))
        fresh.clear()

    base = 64

    def note_row(dx):
        return metas.at[lax.rem(x + dx + SIDE, SIDE), z]

    def note_column(dz):
        return metas.at[:, lax.rem(z + dz + SIDE, SIDE)]

    def note_wait(ref, arrival):
        link.arrive(ref, arrival, neighbour(0, 1))

    def bundle_of(slot, to):
        at = place(to)
        return helps.at[at // SIDE, :, 0] if slot == 0 else helps.at[:, lax.rem(at, SIDE), 1]

    def pair_of(slot, to, low):
        at = place(to)
        part = pl.ds(low, 2)
        return helps.at[at // SIDE, part, 0] if slot == 0 else helps.at[part, lax.rem(at, SIDE), 1]

    def final(slot, along, across):
        return arrived.at[slot, along % SIDE, across % SIDE - 1]

    def arrival(slot, kind):
        return 79 + slot * 28 + kind

    def target(slot, way):
        axis = 1 - slot
        at = place(step(axis, way))
        return lax.rem(at, SIDE) if axis == 1 else at // SIDE

    def far_pairs(slot):
        for way, low in ((1, 0), (-1, 2)):
            k = 0 if way > 0 else 1
            link.start(
                pair_of(slot, step(slot, 2), low), passing.at[slot, k], arrival(slot, k),
                neighbour(slot, way),
            )

    def bundle(slot):
        for way in (1, -1):
            link.start(
                bundle_of(slot, step(slot, way)), first.at[slot, -way % SIDE],
                arrival(slot, 2 + (0 if way > 0 else 1)), neighbour(slot, way),
            )

    def relay(slot):
        for way, low in ((1, 0), (-1, 2)):
            k = 0 if way > 0 else 1
            note_wait(passing.at[slot, k], arrival(slot, k))
            link.start(
                passing.at[slot, k], first.at[slot, 2, pl.ds(low, 2)], arrival(slot, 4 + k),
                neighbour(slot, way),
            )

    def direct(slot, along):
        for way in (1, -1):
            link.start(
                first.at[slot, along % SIDE, target(slot, way)], final(slot, along, -way),
                arrival(slot, 6 + (along % SIDE) * 4 + (-way) % SIDE), neighbour(1 - slot, way),
            )

    by = {0: 1, 1: 1, 3: -1, 2: -1}

    def detour(slot, along):
        way = by[along % SIDE]
        link.start(
            first.at[slot, along % SIDE, target(slot, 2)], second.at[slot, along % SIDE],
            arrival(slot, 22 + along % SIDE), neighbour(1 - slot, way),
        )

    def hand_on(slot, along):
        way = by[along % SIDE]
        note_wait(second.at[slot, along % SIDE], arrival(slot, 22 + along % SIDE))
        link.start(
            second.at[slot, along % SIDE], final(slot, along, 2),
            arrival(slot, 6 + (along % SIDE) * 4 + 2), neighbour(1 - slot, way),
        )

    def bundle_wait(slot, way):
        k = 0 if way > 0 else 1
        note_wait(first.at[slot, -way % SIDE], arrival(slot, 2 + k))

    slots = (0, 1)
    early = len(HELP_ORDER) - LATE

    def rim(has, pieces, start):
        @pl.when(has)
        def _():
            for piece in pieces:
                rim_copy(piece).wait_recv()
            for k in range(RIM // UNIT):
                split_unit(start + k * UNIT)

        @pl.when(jnp.logical_not(has))
        def _():
            ext_parts[start : start + RIM] = jnp.zeros((RIM,) + ext_parts.shape[1:], jnp.bfloat16)

    def noted(k, slot):
        along, across = HELP_ORDER[k]
        dx, dz = (along, across) if slot == 0 else (across, along)
        sx, sz = lax.rem(x + dx, SIDE), lax.rem(z + dz, SIDE)
        return [notes[sx, sz, kind, 0, n * 2 + slot] for kind in range(3)]

    def list_rows(low, high, lines, k):
        spots = lax.broadcasted_iota(jnp.int32, (1, terms.shape[0]), 1)
        rows, load = jnp.full_like(spots, blocks), jnp.zeros_like(spots)
        for each in range(low, high):
            for slot in slots:
                col, row, live = noted(each, slot)
                here = spots == (each - low) * 2 + slot
                rows = jnp.where(here, row, rows)
                load = jnp.where(here, col * 2 + live, load)
        order_table(load, rows, table)
        return fetch(table, lines, k)

    queues = gather_queues()
    turns = len(queues[0][2])
    for turn in range(turns):
        for axis, way, queue, _ in queues:
            origin, sub = queue[turn]
            need(origin, sub)
            seen = (origin[0] - step(axis, way)[0], origin[1] - step(axis, way)[1])
            link.start(
                quarter(origin, sub) if any(origin) else sims.at[pl.ds(sub * UNIT, UNIT)],
                quarter(origin, sub),
                unit_id(seen, sub),
                neighbour(axis, way),
            )
        if turn == 0:
            mine = fetch(sims, ext.at[pl.ds(RIM + n * blocks, blocks)], 0)
            told = [
                fetch(ref, metas.at[x, z, k], 1 + k)
                for k, ref in enumerate((help_cols, help_rows, help_live))
            ]
            vectors = [fetch(own_cols, vec.at[0], 6), fetch(own_rows, vec.at[1], 7)]
            for chunk in (0, 1):
                load(chunk).start()
            bundles = [
                fetch(helps.at[x, :, 0], first.at[0, 0], 4),
                fetch(helps.at[:, z, 1], first.at[1, 0], 5),
            ]
        if turn == 2:
            for copy in told:
                copy.wait()
            link.start(note_row(0), note_row(0), base, neighbour(0, 1))
            link.start(note_row(0), note_row(0), base + 1, neighbour(0, -1))
            mine.wait()
        if turn == 4:
            note_wait(note_row(-1), base)
            note_wait(note_row(1), base + 1)
            link.start(note_row(-1), note_row(-1), base + 2, neighbour(0, 1))
        if turn == 7:
            note_wait(note_row(2), base + 2)
            link.start(note_column(0), note_column(0), base + 3, neighbour(1, 1))
            link.start(note_column(0), note_column(0), base + 4, neighbour(1, -1))
        for slot in slots:
            if turn == 3:
                far_pairs(slot)
            if turn == 6:
                relay(slot)
            if turn == 8:
                bundle(slot)
        if turn < 2:
            continue
        tidy()
        if turn == 2:
            for copy in vectors:
                copy.wait()
            order_table(vec[0], vec[1], table)
            fetch(table, order, 6).wait()
        chunks, spread = n_own // UNIT, turns - 2
        split_tiles(chunks * (turn - 2) // spread, chunks * (turn - 1) // spread)
    note_wait(note_column(-1), base + 3)
    note_wait(note_column(1), base + 4)
    link.start(note_column(-1), note_column(-1), base + 5, neighbour(1, 1))

    for axis, way, _, sub in queues:
        for across in range(SIDE):
            need((-way, across) if axis == 0 else (across, -way), sub)

    def ahead(axis, k):
        lead = SIDE - 1 - z if axis == 0 else SIDE - x
        return lax.rem(lead + k, SIDE)

    for k in range(SIDE):
        for axis, way, _, sub in queues:
            across = ahead(axis, k)
            origin = (-way, across) if axis == 0 else (across, -way)
            seen = (-2, across) if axis == 0 else (across, -2)
            link.start(
                quarter(origin, sub), quarter(origin, sub), unit_id(seen, sub), neighbour(axis, way)
            )
    of_ext = len(link.sent)
    for a in range(SIDE):
        for b in range(SIDE):
            for sub in range(4):
                if not (a == 2 and sub >= 2 or b == 2 and sub < 2):
                    need((a, b), sub)
    tidy()
    for copy in bundles:
        copy.wait()

    for slot in slots:
        for k, low in ((0, 0), (1, 2)):
            note_wait(first.at[slot, 2, pl.ds(low, 2)], arrival(slot, 4 + k))
        for way in (1, -1):
            bundle_wait(slot, way)
    for along in (0, 3, 1, 2):
        for slot in slots:
            detour(slot, along)
    for along in (0, 1, 3, 2):
        for slot in slots:
            direct(slot, along)
    late = len(link.sent)
    note_wait(note_column(2), base + 5)
    fetch(metas, notes, 1).wait()

    for k in range(SIDE):
        for axis, way, _, sub in queues:
            across = ahead(axis, k)
            origin = (2, across) if axis == 0 else (across, 2)
            link.arrive(quarter(origin, sub), unit_id(origin, sub), neighbour(0, 1))
            fresh.append((origin, sub))
        tidy()
        if k == 0:
            help_table = list_rows(0, early, help_order, 2)
        if k == 1:
            help_table.wait()
            late_table = list_rows(early, len(HELP_ORDER), late_order, 3)
    rim(g > 0, (0, 1), 0)
    rim(g < groups - 1, (2, 3), total - RIM)
    for copy in link.sent[:of_ext]:
        copy.wait_send()

    @pl.when(g < groups - 1)
    def _():
        for piece in (0, 1):
            rim_copy(piece).wait_send()

    @pl.when(g > 0)
    def _():
        for piece in (2, 3):
            rim_copy(piece).wait_send()

    def own(low, high):
        def body(k, acc):
            for u in range(UNROLL):
                at = low + k * UNROLL + u
                keep = order[2, at].astype(jnp.float32)
                acc = acc * keep + product(tile_parts[order[0, at]], ext_parts[order[1, at]])
                ext[at] = acc
            return acc

        acc = jnp.zeros(ext.shape[1:], jnp.float32) if low == 0 else ext[low - 1]
        lax.fori_loop(0, (high - low) // UNROLL, body, acc)

    def help_products(low, high):
        for k in range(low, high):
            along, across = HELP_ORDER[k]
            for slot in slots:
                if across:
                    note_wait(final(slot, along, across), arrival(slot, 6 + along * 4 + across))
        for k in range(low, high):
            along, across = HELP_ORDER[k]
            for slot in slots:
                tile = (
                    arrived[slot, along, across - 1]
                    if across
                    else first[slot, along, target(slot, 0)]
                )
                terms[k * 2 + slot] = product(split(tile), ext_parts[noted(k, slot)[0]])

    cut = n_own // 2
    own(0, cut)
    for along in (0, 3, 1, 2):
        for slot in slots:
            hand_on(slot, along)
    own(cut, n_own)

    @pl.loop(0, blocks)
    def _(row):
        sums[row] = ext[order[3, row]] * order[4, row].astype(jnp.float32)

    help_products(0, 4)
    help_products(4, 8)
    help_products(8, 12)
    help_products(12, early)
    acc = jnp.zeros(ext.shape[1:], jnp.float32)
    for at in range(2 * early):
        keep = help_order[2, at].astype(jnp.float32)
        live = jnp.bitwise_and(help_order[1, at], 1).astype(jnp.float32)
        acc = acc * keep + terms[help_order[0, at]] * live
        ext[at] = acc

    @pl.loop(0, blocks)
    def _(row):
        sums[row] += ext[help_order[3, row]] * help_order[4, row].astype(jnp.float32)

    late_table.wait()
    for copy in link.sent[of_ext:late]:
        copy.wait_send()
    for along, across in HELP_ORDER[early:]:
        for slot in slots:
            note_wait(final(slot, along, across), arrival(slot, 6 + along * 4 + across))
    acc = jnp.zeros(ext.shape[1:], jnp.float32)
    for at in range(2 * LATE):
        which, load = late_order[0, at], late_order[1, at]
        tile = arrived[lax.rem(which, 2), 1 + which // 2, 1]
        keep = late_order[2, at].astype(jnp.float32)
        live = jnp.bitwise_and(load, 1).astype(jnp.float32)
        acc = acc * keep + product(split(tile), ext_parts[jnp.right_shift(load, 1)]) * live
        ext[at] = acc

    @pl.loop(0, blocks)
    def _(row):
        sums_out[row] = sums[row] + ext[late_order[3, row]] * late_order[4, row].astype(jnp.float32)

    for copy in link.sent[late:]:
        copy.wait_send()


def local(sims, own_tiles, own_cols, own_rows, help_tiles, help_cols, help_rows, help_live):
    blocks, size = sims.shape[0], sims.shape[1:]
    neighbours = lax.axis_size("nbr")
    helps, owns = help_tiles.shape[0], own_tiles.shape[0]
    extended = blocks * neighbours + 2 * RIM
    parts = (size[0], 2 * size[1])
    any_space = pl.BlockSpec(memory_space=pl.ANY)
    f32, bf16, i32 = jnp.float32, jnp.bfloat16, jnp.int32
    return pl.pallas_call(
        exchange,
        out_shape=pltpu.VMEM(sims.shape, f32),
        in_specs=[any_space] * 8,
        out_specs=pl.BlockSpec(memory_space=pltpu.VMEM),
        scratch_shapes=[
            pltpu.VMEM((extended,) + size, f32),
            pltpu.VMEM((extended,) + parts, bf16),
            pltpu.VMEM((owns,) + parts, bf16),
            pltpu.VMEM((2, UNIT) + size, f32),
            pltpu.VMEM((2, SIDE, SIDE) + size, f32),
            pltpu.VMEM((2, 2, 2) + size, f32),
            pltpu.VMEM((2, SIDE) + size, f32),
            pltpu.VMEM((2, SIDE, SIDE - 1) + size, f32),
            pltpu.VMEM((helps,) + size, f32),
            pltpu.VMEM(sims.shape, f32),
            pltpu.VMEM((SIDE, SIDE, 3, 1, helps), i32),
            pltpu.VMEM((2, 1, owns), i32),
            pltpu.VMEM((8, 256), i32),
            pltpu.SMEM((8, 256), i32),
            pltpu.SMEM((8, 256), i32),
            pltpu.SMEM((8, 256), i32),
            pltpu.SMEM((SIDE, SIDE, 3, 1, helps), i32),
            pltpu.SemaphoreType.DMA((160,)),
            pltpu.SemaphoreType.DMA((160,)),
            pltpu.SemaphoreType.DMA((4,)),
            pltpu.SemaphoreType.DMA((4,)),
            pltpu.SemaphoreType.DMA((8,)),
            pltpu.SemaphoreType.DMA((2,)),
        ],
        compiler_params=pltpu.CompilerParams(
            collective_id=0, has_side_effects=True, vmem_limit_bytes=57 * 2**20
        ),
        name="exchange",
    )(
        sims,
        help_tiles.reshape((SIDE, SIDE, 2) + size),
        own_tiles,
        *(v.reshape(1, -1) for v in (own_cols, own_rows, help_cols, help_rows, help_live)),
    )


def solution(mesh):
    whole, flat = P(("grp", "nbr"), None, None), P(("grp", "nbr"))
    placed = (whole, whole, flat, flat, whole, flat, flat, flat)
    return jax.shard_map(local, mesh=mesh, in_specs=placed, out_specs=whole, check_vma=False)
```

```python
import jax
import jax.numpy as jnp
from jax import lax
from jax.experimental import pallas as pl
from jax.experimental.pallas import tpu as pltpu
from jax.sharding import PartitionSpec as P

RIM = 8
UNIT = 4
SIDE = 4
UNROLL = 16
MESH = pl.DeviceIdType.MESH
GATHER, HELPER, NOTES = 0, 1, 2


def wrap(value):
    return (value + SIDE) % SIDE if isinstance(value, int) else lax.rem(value + SIDE, SIDE)


def gather_queues():
    queues = []
    for axis in (0, 1):
        for way in (1, -1):
            near, far = ((0, 1), (2, 3)) if axis == 0 else ((2, 3), (0, 1))
            if way < 0:
                near, far = near[::-1], far[::-1]

            def at(along, across, axis=axis):
                return (along, across) if axis == 0 else (across, along)

            queue = [
                (at(0, 0), near[0]),
                (at(0, 0), near[1]),
                (at(0, 0), far[0]),
                (at(-way, 0), near[0]),
                (at(0, 0), far[1]),
                (at(0, -1), far[0]),
                (at(0, 1), far[0]),
                (at(0, -1), far[1]),
                (at(0, 1), far[1]),
                (at(0, 2), far[0]),
                (at(0, 2), far[1]),
            ]
            queues.append((axis, way, queue, far[0]))
    return queues


class Link:
    def __init__(self, send, recv):
        self.send, self.recv = send, recv

    def start(self, src, dst, sent, arrival, device):
        pltpu.make_async_remote_copy(
            src_ref=src,
            dst_ref=dst,
            send_sem=self.send.at[sent],
            recv_sem=self.recv.at[arrival],
            device_id=device,
            device_id_type=MESH,
        ).start()

    def whole(self, ref, sent, arrival, device):
        return pltpu.make_async_remote_copy(
            src_ref=ref,
            dst_ref=ref,
            send_sem=self.send.at[sent],
            recv_sem=self.recv.at[arrival],
            device_id=device,
            device_id_type=MESH,
        )


def split(value):
    high = value.astype(jnp.bfloat16)
    low = (value - high.astype(jnp.float32)).astype(jnp.bfloat16)
    return jnp.concatenate([high, low], axis=1)


def product(tile, block):
    both = jnp.dot(
        tile, jnp.concatenate([block, block], axis=0), preferred_element_type=jnp.float32
    )
    half = both.shape[1] // 2
    return both[:, :half] + both[:, half:]


def order_table(cols, rows, table):
    count = rows.shape[1]
    table[...] = jnp.zeros_like(table)
    line = lax.broadcasted_iota(jnp.int32, (count, count), 1)
    deep = lax.broadcasted_iota(jnp.int32, (count, count), 0)

    def upright(value):
        return jnp.sum(jnp.where(line == deep, value, 0), axis=1, keepdims=True)

    key = rows * 256 + line[:1]
    key_up, col_up = upright(key), upright(cols)
    row_up = jnp.right_shift(key_up, 8)
    rank = jnp.sum((key < key_up).astype(jnp.int32), axis=1, keepdims=True)
    here = rank == line
    before = rank == line - 1
    row_at = jnp.sum(jnp.where(here, row_up, 0), axis=0, keepdims=True)
    row_before = jnp.sum(jnp.where(before, row_up + 1, 0), axis=0, keepdims=True) - 1
    table[0:1, :count] = jnp.sum(jnp.where(here, deep, 0), axis=0, keepdims=True)
    table[1:2, :count] = jnp.sum(jnp.where(here, col_up, 0), axis=0, keepdims=True)
    table[2:3, :count] = (row_at == row_before).astype(jnp.int32)
    upto = jnp.sum((row_up <= line).astype(jnp.int32), axis=0, keepdims=True)
    table[3:4, :count] = jnp.maximum(upto - 1, 0)
    table[4:5, :count] = jnp.minimum(
        jnp.sum((row_up == line).astype(jnp.int32), axis=0, keepdims=True), 1
    )


HELP_ORDER = (
    [(0, 0), (1, 0), (3, 0), (2, 0), (0, 1), (0, 3), (1, 1), (1, 3)]
    + [(3, 1), (3, 3), (2, 1), (2, 3), (0, 2), (3, 2), (1, 2), (2, 2)]
)
LATE = 2


def exchange(
    sims, helps, tiles, own_cols, own_rows, help_cols, help_rows, help_live,
    sums_out,
    ext, ext_parts, tile_parts, stage, first, passing, second, arrived, terms, sums,
    metas, vec, table, order, help_order, late_order, notes,
    send, recv, rim_send, rim_recv, local_sem, stage_sem,
):
    n, g = lax.axis_index("nbr"), lax.axis_index("grp")
    groups = lax.axis_size("grp")
    x, z = n // SIDE, lax.rem(n, SIDE)
    blocks = sims.shape[0]
    total = ext.shape[0]
    n_own = tiles.shape[0]
    last = SIDE * SIDE - 1
    helps_dev = terms.shape[0]

    def place(origin):
        return lax.rem(x + origin[0] + SIDE, SIDE) * SIDE + lax.rem(z + origin[1] + SIDE, SIDE)

    def step(axis, way):
        return (way, 0) if axis == 0 else (0, way)

    def neighbour(axis, way):
        return {"nbr": place(step(axis, way))}

    barrier = pltpu.get_barrier_semaphore()
    for axis in (0, 1):
        for way in (1, -1):
            pl.semaphore_signal(barrier, inc=1, device_id=neighbour(axis, way), device_id_type=MESH)

    @pl.when(g > 0)
    def _():
        pl.semaphore_signal(barrier, inc=1, device_id={"grp": g - 1}, device_id_type=MESH)

    @pl.when(g < groups - 1)
    def _():
        pl.semaphore_signal(barrier, inc=1, device_id={"grp": g + 1}, device_id_type=MESH)

    def fetch(src, dst, k):
        copy = pltpu.make_async_copy(src, dst, local_sem.at[k])
        copy.start()
        return copy

    def load(chunk):
        at = lax.rem(chunk, 2)
        return pltpu.make_async_copy(
            tiles.at[pl.ds(chunk * UNIT, UNIT)], stage.at[at], stage_sem.at[at]
        )

    pl.semaphore_wait(
        barrier, 4 + (g > 0).astype(jnp.int32) + (g < groups - 1).astype(jnp.int32)
    )
    link = Link(send, recv)

    def split_unit(start):
        @pl.loop(0, UNIT)
        def _(k):
            ext_parts[start + k] = split(ext[start + k])

    def split_tiles(low, high):
        @pl.loop(low, high)
        def _(chunk):
            load(chunk).wait()
            at = lax.rem(chunk, 2)

            @pl.loop(0, UNIT)
            def _(k):
                tile_parts[chunk * UNIT + k] = split(stage[at, k])

            @pl.when(chunk + 2 < n_own // UNIT)
            def _():
                load(chunk + 2).start()

    def rim_copy(piece):
        up = piece < 2
        src = total - 2 * RIM + piece * UNIT if up else RIM + (piece - 2) * UNIT
        dst = piece * UNIT if up else total - RIM + (piece - 2) * UNIT
        peer = lax.rem(g + 1, groups) if up else lax.rem(g + groups - 1, groups)
        return pltpu.make_async_remote_copy(
            src_ref=ext.at[pl.ds(src, UNIT)], dst_ref=ext.at[pl.ds(dst, UNIT)],
            send_sem=rim_send.at[piece], recv_sem=rim_recv.at[piece],
            device_id={"grp": peer}, device_id_type=MESH,
        )

    def rim_leaves(origin, sub):
        at = place(origin)
        sends = (at == last) & (g < groups - 1) if sub >= 2 else (at == 0) & (g > 0)

        @pl.when(sends)
        def _():
            rim_copy(sub - 2 if sub >= 2 else sub + 2).start()

    def base_of(origin, sub):
        return RIM + place(origin) * blocks + sub * UNIT

    def quarter(origin, sub):
        return ext.at[pl.ds(base_of(origin, sub), UNIT)]

    queues = gather_queues()
    turns = len(queues[0][2])
    groups_of = {}
    for axis, way, queue, _ in queues:
        for turn, (origin, sub) in enumerate(queue):
            dx, dz = step(axis, way)
            groups_of[wrap(origin[0] - dx), wrap(origin[1] - dz), sub] = turn
    here = set()
    fresh = [((0, 0), sub) for sub in range(4)]

    def arrive(ref, arrival):
        link.whole(ref, 0, arrival, neighbour(0, 1)).wait_recv()

    def need(origin, sub):
        turn = groups_of.get((wrap(origin[0]), wrap(origin[1]), sub))
        if turn is None or turn in here:
            return
        here.add(turn)
        fresh.extend(((a, b), each) for (a, b, each), when in groups_of.items() if when == turn)
        arrive(ext.at[pl.ds(0, len(queues) * UNIT)], turn)

    def tidy():
        for origin, sub in fresh:
            rim_leaves(origin, sub)
        for origin, sub in fresh:
            split_unit(base_of(origin, sub))
        fresh.clear()

    base = turns + SIDE

    def note_row(dx):
        return metas.at[lax.rem(x + dx + SIDE, SIDE), z]

    def note_column(dz):
        return metas.at[:, lax.rem(z + dz + SIDE, SIDE)]

    def note_wait(ref, k):
        arrive(ref, base + k)

    def bundle_of(slot, to):
        at = place(to)
        return helps.at[at // SIDE, :, 0] if slot == 0 else helps.at[:, lax.rem(at, SIDE), 1]

    def pair_of(slot, to, low):
        at = place(to)
        part = pl.ds(low, 2)
        return helps.at[at // SIDE, part, 0] if slot == 0 else helps.at[part, lax.rem(at, SIDE), 1]

    def final(slot, along, across):
        return arrived.at[slot, along % SIDE, across % SIDE - 1]

    passed, begun, turned, ended = base + 6, base + 7, base + 8, base + 10

    def target(slot, way):
        axis = 1 - slot
        at = place(step(axis, way))
        return lax.rem(at, SIDE) if axis == 1 else at // SIDE

    def far_pairs(slot):
        for way, low in ((1, 0), (-1, 2)):
            link.start(
                pair_of(slot, step(slot, 2), low), passing.at[slot, 0 if way > 0 else 1],
                HELPER, passed, neighbour(slot, way),
            )

    def bundle(slot):
        for way in (1, -1):
            link.start(
                bundle_of(slot, step(slot, way)), first.at[slot, -way % SIDE],
                HELPER, begun, neighbour(slot, way),
            )

    def relay(slot):
        for way, low in ((1, 0), (-1, 2)):
            link.start(
                passing.at[slot, 0 if way > 0 else 1], first.at[slot, 2, pl.ds(low, 2)],
                HELPER, begun, neighbour(slot, way),
            )

    def direct(slot, along):
        for way in (1, -1):
            link.start(
                first.at[slot, along, target(slot, way)], final(slot, along, -way),
                HELPER, ended + along // 2, neighbour(1 - slot, way),
            )

    by = {0: 1, 1: 1, 3: -1, 2: -1}
    soon = (0, 3)

    def detour(slot, along):
        link.start(
            first.at[slot, along, target(slot, 2)], second.at[slot, along],
            HELPER, turned + (0 if along in soon else 1), neighbour(1 - slot, by[along]),
        )

    def hand_on(slot, along):
        link.start(
            second.at[slot, along], final(slot, along, 2),
            HELPER, ended + (2 if along in soon else 3), neighbour(1 - slot, by[along]),
        )

    slots = (0, 1)
    early = len(HELP_ORDER) - LATE

    def rim(has, pieces, start):
        @pl.when(has)
        def _():
            for piece in pieces:
                rim_copy(piece).wait_recv()
            for k in range(RIM // UNIT):
                split_unit(start + k * UNIT)

        @pl.when(jnp.logical_not(has))
        def _():
            ext_parts[start : start + RIM] = jnp.zeros((RIM,) + ext_parts.shape[1:], jnp.bfloat16)

    def noted(k, slot):
        along, across = HELP_ORDER[k]
        dx, dz = (along, across) if slot == 0 else (across, along)
        sx, sz = lax.rem(x + dx, SIDE), lax.rem(z + dz, SIDE)
        return [notes[sx, sz, kind, 0, n * 2 + slot] for kind in range(3)]

    def list_rows(low, high, lines, k):
        spots = lax.broadcasted_iota(jnp.int32, (1, terms.shape[0]), 1)
        rows, load = jnp.full_like(spots, blocks), jnp.zeros_like(spots)
        for each in range(low, high):
            for slot in slots:
                col, row, live = noted(each, slot)
                here = spots == (each - low) * 2 + slot
                rows = jnp.where(here, row, rows)
                load = jnp.where(here, col * 2 + live, load)
        order_table(load, rows, table)
        return fetch(table, lines, k)

    for turn in range(turns):
        for axis, way, queue, _ in queues:
            origin, sub = queue[turn]
            need(origin, sub)
            link.start(
                quarter(origin, sub) if any(origin) else sims.at[pl.ds(sub * UNIT, UNIT)],
                quarter(origin, sub),
                GATHER,
                turn,
                neighbour(axis, way),
            )
        if turn == 0:
            mine = fetch(sims, ext.at[pl.ds(RIM + n * blocks, blocks)], 0)
            told = [
                fetch(ref, metas.at[x, z, k], 1 + k)
                for k, ref in enumerate((help_cols, help_rows, help_live))
            ]
            vectors = [fetch(own_cols, vec.at[0], 6), fetch(own_rows, vec.at[1], 7)]
            for chunk in (0, 1):
                load(chunk).start()
            bundles = [
                fetch(helps.at[x, :, 0], first.at[0, 0], 4),
                fetch(helps.at[:, z, 1], first.at[1, 0], 5),
            ]
        if turn == 2:
            for copy in told:
                copy.wait()
            link.start(note_row(0), note_row(0), NOTES + 0, base + 0, neighbour(0, 1))
            link.start(note_row(0), note_row(0), NOTES + 1, base + 1, neighbour(0, -1))
            mine.wait()
        if turn == 4:
            note_wait(note_row(-1), 0)
            note_wait(note_row(1), 1)
            link.start(note_row(-1), note_row(-1), NOTES + 2, base + 2, neighbour(0, 1))
        if turn == 7:
            note_wait(note_row(2), 2)
            link.start(note_column(0), note_column(0), NOTES + 3, base + 3, neighbour(1, 1))
            link.start(note_column(0), note_column(0), NOTES + 4, base + 4, neighbour(1, -1))
        for slot in slots:
            if turn == 3:
                far_pairs(slot)
            if turn == 6:
                if slot == 0:
                    arrive(passing, passed)
                relay(slot)
            if turn == 8:
                bundle(slot)
        if turn < 2:
            continue
        tidy()
        if turn == 2:
            for copy in vectors:
                copy.wait()
            order_table(vec[0], vec[1], table)
            fetch(table, order, 6).wait()
        chunks, spread = n_own // UNIT, turns - 2
        split_tiles(chunks * (turn - 2) // spread, chunks * (turn - 1) // spread)
    note_wait(note_column(-1), 3)
    note_wait(note_column(1), 4)
    link.start(note_column(-1), note_column(-1), NOTES + 5, base + 5, neighbour(1, 1))

    for axis, way, _, sub in queues:
        for across in range(SIDE):
            need((-way, across) if axis == 0 else (across, -way), sub)

    def ahead(axis, k):
        lead = SIDE - 1 - z if axis == 0 else SIDE - x
        return lax.rem(lead + k, SIDE)

    for k in range(SIDE):
        for axis, way, _, sub in queues:
            across = ahead(axis, k)
            origin = (-way, across) if axis == 0 else (across, -way)
            link.start(
                quarter(origin, sub), quarter(origin, sub), GATHER, turns + k, neighbour(axis, way)
            )
    for a in range(SIDE):
        for b in range(SIDE):
            for sub in range(4):
                if not (a == 2 and sub >= 2 or b == 2 and sub < 2):
                    need((a, b), sub)
    tidy()
    for copy in bundles:
        copy.wait()

    arrive(first.at[:, pl.ds(1, SIDE - 1)], begun)
    for along in (0, 3, 1, 2):
        for slot in slots:
            detour(slot, along)
    for along in (0, 1, 3, 2):
        for slot in slots:
            direct(slot, along)
    note_wait(note_column(2), 5)
    fetch(metas, notes, 1).wait()

    for k in range(SIDE):
        for axis, way, _, sub in queues:
            across = ahead(axis, k)
            origin = (2, across) if axis == 0 else (across, 2)
            fresh.append((origin, sub))
        arrive(ext.at[pl.ds(0, len(queues) * UNIT)], turns + k)
        tidy()
        if k == 0:
            help_table = list_rows(0, early, help_order, 2)
        if k == 1:
            help_table.wait()
            late_table = list_rows(early, len(HELP_ORDER), late_order, 3)
    rim(g > 0, (0, 1), 0)
    rim(g < groups - 1, (2, 3), total - RIM)
    link.whole(ext.at[pl.ds(0, len(queues) * (turns + SIDE) * UNIT)], GATHER, 0, neighbour(0, 1)).wait_send()

    @pl.when(g < groups - 1)
    def _():
        for piece in (0, 1):
            rim_copy(piece).wait_send()

    @pl.when(g > 0)
    def _():
        for piece in (2, 3):
            rim_copy(piece).wait_send()

    def own(low, high):
        def body(k, acc):
            for u in range(UNROLL):
                at = low + k * UNROLL + u
                keep = order[2, at].astype(jnp.float32)
                acc = acc * keep + product(tile_parts[order[0, at]], ext_parts[order[1, at]])
                ext[at] = acc
            return acc

        acc = jnp.zeros(ext.shape[1:], jnp.float32) if low == 0 else ext[low - 1]
        lax.fori_loop(0, (high - low) // UNROLL, body, acc)

    def help_products(low, high):
        for k in range(low, high):
            along, across = HELP_ORDER[k]
            for slot in slots:
                tile = (
                    arrived[slot, along, across - 1]
                    if across
                    else first[slot, along, target(slot, 0)]
                )
                terms[k * 2 + slot] = product(split(tile), ext_parts[noted(k, slot)[0]])

    cut = n_own // 2
    own(0, cut)
    for k, part in enumerate((soon, (1, 2))):
        arrive(second.at[0], turned + k)
        for along in part:
            for slot in slots:
                hand_on(slot, along)
    own(cut, n_own)

    @pl.loop(0, blocks)
    def _(row):
        sums[row] = ext[order[3, row]] * order[4, row].astype(jnp.float32)

    help_products(0, 4)
    arrive(first.at[0, pl.ds(0, 2)], ended)
    help_products(4, 8)
    arrive(first.at[0, pl.ds(0, 2)], ended + 1)
    help_products(8, 12)
    arrive(second.at[0], ended + 2)
    help_products(12, early)
    acc = jnp.zeros(ext.shape[1:], jnp.float32)
    for at in range(2 * early):
        keep = help_order[2, at].astype(jnp.float32)
        live = jnp.bitwise_and(help_order[1, at], 1).astype(jnp.float32)
        acc = acc * keep + terms[help_order[0, at]] * live
        ext[at] = acc

    @pl.loop(0, blocks)
    def _(row):
        sums[row] += ext[help_order[3, row]] * help_order[4, row].astype(jnp.float32)

    late_table.wait()
    for k in range(3):
        link.whole(note_row(0), NOTES + k, 0, neighbour(0, 1)).wait_send()
        link.whole(note_column(0), NOTES + 3 + k, 0, neighbour(0, 1)).wait_send()
    arrive(second.at[0], ended + 3)
    acc = jnp.zeros(ext.shape[1:], jnp.float32)
    for at in range(2 * LATE):
        which, load = late_order[0, at], late_order[1, at]
        tile = arrived[lax.rem(which, 2), 1 + which // 2, 1]
        keep = late_order[2, at].astype(jnp.float32)
        live = jnp.bitwise_and(load, 1).astype(jnp.float32)
        acc = acc * keep + product(split(tile), ext_parts[jnp.right_shift(load, 1)]) * live
        ext[at] = acc

    @pl.loop(0, blocks)
    def _(row):
        sums_out[row] = sums[row] + ext[late_order[3, row]] * late_order[4, row].astype(jnp.float32)

    link.whole(ext.at[pl.ds(0, 2 * helps_dev)], HELPER, 0, neighbour(0, 1)).wait_send()


def local(sims, own_tiles, own_cols, own_rows, help_tiles, help_cols, help_rows, help_live):
    blocks, size = sims.shape[0], sims.shape[1:]
    neighbours = lax.axis_size("nbr")
    helps, owns = help_tiles.shape[0], own_tiles.shape[0]
    extended = blocks * neighbours + 2 * RIM
    parts = (size[0], 2 * size[1])
    any_space = pl.BlockSpec(memory_space=pl.ANY)
    f32, bf16, i32 = jnp.float32, jnp.bfloat16, jnp.int32
    return pl.pallas_call(
        exchange,
        out_shape=pltpu.VMEM(sims.shape, f32),
        in_specs=[any_space] * 8,
        out_specs=pl.BlockSpec(memory_space=pltpu.VMEM),
        scratch_shapes=[
            pltpu.VMEM((extended,) + size, f32),
            pltpu.VMEM((extended,) + parts, bf16),
            pltpu.VMEM((owns,) + parts, bf16),
            pltpu.VMEM((2, UNIT) + size, f32),
            pltpu.VMEM((2, SIDE, SIDE) + size, f32),
            pltpu.VMEM((2, 2, 2) + size, f32),
            pltpu.VMEM((2, SIDE) + size, f32),
            pltpu.VMEM((2, SIDE, SIDE - 1) + size, f32),
            pltpu.VMEM((helps,) + size, f32),
            pltpu.VMEM(sims.shape, f32),
            pltpu.VMEM((SIDE, SIDE, 3, 1, helps), i32),
            pltpu.VMEM((2, 1, owns), i32),
            pltpu.VMEM((8, 256), i32),
            pltpu.SMEM((8, 256), i32),
            pltpu.SMEM((8, 256), i32),
            pltpu.SMEM((8, 256), i32),
            pltpu.SMEM((SIDE, SIDE, 3, 1, helps), i32),
            pltpu.SemaphoreType.DMA((8,)),
            pltpu.SemaphoreType.DMA((29,)),
            pltpu.SemaphoreType.DMA((4,)),
            pltpu.SemaphoreType.DMA((4,)),
            pltpu.SemaphoreType.DMA((8,)),
            pltpu.SemaphoreType.DMA((2,)),
        ],
        compiler_params=pltpu.CompilerParams(
            collective_id=0, has_side_effects=True, vmem_limit_bytes=57 * 2**20
        ),
        name="exchange",
    )(
        sims,
        help_tiles.reshape((SIDE, SIDE, 2) + size),
        own_tiles,
        *(v.reshape(1, -1) for v in (own_cols, own_rows, help_cols, help_rows, help_live)),
    )


def solution(mesh):
    whole, flat = P(("grp", "nbr"), None, None), P(("grp", "nbr"))
    placed = (whole, whole, flat, flat, whole, flat, flat, flat)
    return jax.shard_map(local, mesh=mesh, in_specs=placed, out_specs=whole, check_vma=False)
```

```python
import jax
import jax.numpy as jnp
from jax import lax
from jax.experimental import pallas as pl
from jax.experimental.pallas import tpu as pltpu
from jax.sharding import PartitionSpec as P

RIM = 8
UNIT = 4
SIDE = 4
UNROLL = 16
MESH = pl.DeviceIdType.MESH
GATHER, HELPER, NOTES = 0, 1, 2


def wrap(value):
    return (value + SIDE) % SIDE if isinstance(value, int) else lax.rem(value + SIDE, SIDE)


def gather_queues():
    queues = []
    for axis in (0, 1):
        for way in (1, -1):
            near, far = ((0, 1), (2, 3)) if axis == 0 else ((2, 3), (0, 1))
            if way < 0:
                near, far = near[::-1], far[::-1]

            def at(along, across, axis=axis):
                return (along, across) if axis == 0 else (across, along)

            queue = [
                (at(0, 0), near[0]),
                (at(0, 0), near[1]),
                (at(0, 0), far[0]),
                (at(-way, 0), near[0]),
                (at(0, 0), far[1]),
                (at(0, -1), far[0]),
                (at(0, 1), far[0]),
                (at(0, -1), far[1]),
                (at(0, 1), far[1]),
                (at(0, 2), far[0]),
                (at(0, 2), far[1]),
            ]
            queues.append((axis, way, queue, far[0]))
    return queues


class Link:
    def __init__(self, send, recv):
        self.send, self.recv = send, recv

    def start(self, src, dst, sent, arrival, device):
        pltpu.make_async_remote_copy(
            src_ref=src,
            dst_ref=dst,
            send_sem=self.send.at[sent],
            recv_sem=self.recv.at[arrival],
            device_id=device,
            device_id_type=MESH,
        ).start()

    def whole(self, ref, sent, arrival, device):
        return pltpu.make_async_remote_copy(
            src_ref=ref,
            dst_ref=ref,
            send_sem=self.send.at[sent],
            recv_sem=self.recv.at[arrival],
            device_id=device,
            device_id_type=MESH,
        )


def split(value):
    high = value.astype(jnp.bfloat16)
    low = (value - high.astype(jnp.float32)).astype(jnp.bfloat16)
    return jnp.concatenate([high, low], axis=1)


def product(tile, block):
    both = jnp.dot(
        tile, jnp.concatenate([block, block], axis=0), preferred_element_type=jnp.float32
    )
    half = both.shape[1] // 2
    return both[:, :half] + both[:, half:]


def order_table(cols, rows, table):
    count = rows.shape[1]
    table[...] = jnp.zeros_like(table)
    line = lax.broadcasted_iota(jnp.int32, (count, count), 1)
    deep = lax.broadcasted_iota(jnp.int32, (count, count), 0)

    def upright(value):
        return jnp.sum(jnp.where(line == deep, value, 0), axis=1, keepdims=True)

    key = rows * 256 + line[:1]
    key_up, col_up = upright(key), upright(cols)
    row_up = jnp.right_shift(key_up, 8)
    rank = jnp.sum((key < key_up).astype(jnp.int32), axis=1, keepdims=True)
    here = rank == line
    before = rank == line - 1
    row_at = jnp.sum(jnp.where(here, row_up, 0), axis=0, keepdims=True)
    row_before = jnp.sum(jnp.where(before, row_up + 1, 0), axis=0, keepdims=True) - 1
    table[0:1, :count] = jnp.sum(jnp.where(here, deep, 0), axis=0, keepdims=True)
    table[1:2, :count] = jnp.sum(jnp.where(here, col_up, 0), axis=0, keepdims=True)
    table[2:3, :count] = (row_at == row_before).astype(jnp.int32)
    upto = jnp.sum((row_up <= line).astype(jnp.int32), axis=0, keepdims=True)
    table[3:4, :count] = jnp.maximum(upto - 1, 0)
    table[4:5, :count] = jnp.minimum(
        jnp.sum((row_up == line).astype(jnp.int32), axis=0, keepdims=True), 1
    )


HELP_ORDER = (
    [(0, 0), (1, 0), (3, 0), (2, 0), (0, 1), (0, 3), (1, 1), (1, 3)]
    + [(3, 1), (3, 3), (2, 1), (2, 3), (0, 2), (3, 2), (1, 2), (2, 2)]
)
LATE = 2


def exchange(
    sims, helps, tiles, own_cols, own_rows, help_cols, help_rows, help_live,
    sums_out,
    ext, ext_parts, tile_parts, stage, first, passing, second, arrived, terms, sums,
    metas, vec, table, order, help_order, late_order, notes,
    send, recv, rim_send, rim_recv, local_sem, stage_sem,
):
    n, g = lax.axis_index("nbr"), lax.axis_index("grp")
    groups = lax.axis_size("grp")
    x, z = n // SIDE, lax.rem(n, SIDE)
    blocks = sims.shape[0]
    total = ext.shape[0]
    n_own = tiles.shape[0]
    last = SIDE * SIDE - 1
    helps_dev = terms.shape[0]

    def place(origin):
        return lax.rem(x + origin[0] + SIDE, SIDE) * SIDE + lax.rem(z + origin[1] + SIDE, SIDE)

    def step(axis, way):
        return (way, 0) if axis == 0 else (0, way)

    def neighbour(axis, way):
        return {"nbr": place(step(axis, way))}

    barrier = pltpu.get_barrier_semaphore()
    for axis in (0, 1):
        for way in (1, -1):
            pl.semaphore_signal(barrier, inc=1, device_id=neighbour(axis, way), device_id_type=MESH)

    @pl.when(g > 0)
    def _():
        pl.semaphore_signal(barrier, inc=1, device_id={"grp": g - 1}, device_id_type=MESH)

    @pl.when(g < groups - 1)
    def _():
        pl.semaphore_signal(barrier, inc=1, device_id={"grp": g + 1}, device_id_type=MESH)

    def fetch(src, dst, k):
        copy = pltpu.make_async_copy(src, dst, local_sem.at[k])
        copy.start()
        return copy

    def load(chunk):
        at = lax.rem(chunk, 2)
        return pltpu.make_async_copy(
            tiles.at[pl.ds(chunk * UNIT, UNIT)], stage.at[at], stage_sem.at[at]
        )

    pl.semaphore_wait(
        barrier, 4 + (g > 0).astype(jnp.int32) + (g < groups - 1).astype(jnp.int32)
    )
    link = Link(send, recv)

    def split_unit(start):
        @pl.loop(0, UNIT)
        def _(k):
            ext_parts[start + k] = split(ext[start + k])

    def split_tiles(low, high):
        @pl.loop(low, high)
        def _(chunk):
            load(chunk).wait()
            at = lax.rem(chunk, 2)

            @pl.loop(0, UNIT)
            def _(k):
                tile_parts[chunk * UNIT + k] = split(stage[at, k])

            @pl.when(chunk + 2 < n_own // UNIT)
            def _():
                load(chunk + 2).start()

    def rim_copy(piece):
        up = piece < 2
        src = total - 2 * RIM + piece * UNIT if up else RIM + (piece - 2) * UNIT
        dst = piece * UNIT if up else total - RIM + (piece - 2) * UNIT
        peer = lax.rem(g + 1, groups) if up else lax.rem(g + groups - 1, groups)
        return pltpu.make_async_remote_copy(
            src_ref=ext.at[pl.ds(src, UNIT)], dst_ref=ext.at[pl.ds(dst, UNIT)],
            send_sem=rim_send.at[piece // 2], recv_sem=rim_recv.at[piece // 2],
            device_id={"grp": peer}, device_id_type=MESH,
        )

    def rim_whole(up):
        ref = ext.at[pl.ds(0 if up else total - RIM, RIM)]
        return pltpu.make_async_remote_copy(
            src_ref=ref, dst_ref=ref,
            send_sem=rim_send.at[0 if up else 1], recv_sem=rim_recv.at[0 if up else 1],
            device_id=neighbour(0, 1), device_id_type=MESH,
        )

    def rim_leaves(origin, sub):
        at = place(origin)
        sends = (at == last) & (g < groups - 1) if sub >= 2 else (at == 0) & (g > 0)

        @pl.when(sends)
        def _():
            rim_copy(sub - 2 if sub >= 2 else sub + 2).start()

    def base_of(origin, sub):
        return RIM + place(origin) * blocks + sub * UNIT

    def quarter(origin, sub):
        return ext.at[pl.ds(base_of(origin, sub), UNIT)]

    queues = gather_queues()
    turns = len(queues[0][2])
    groups_of = {}
    for axis, way, queue, _ in queues:
        for turn, (origin, sub) in enumerate(queue):
            dx, dz = step(axis, way)
            groups_of[wrap(origin[0] - dx), wrap(origin[1] - dz), sub] = turn
    here = set()
    fresh = [((0, 0), sub) for sub in range(4)]

    def arrive(ref, arrival):
        link.whole(ref, 0, arrival, neighbour(0, 1)).wait_recv()

    def need(origin, sub):
        turn = groups_of.get((wrap(origin[0]), wrap(origin[1]), sub))
        if turn is None or turn in here:
            return
        here.add(turn)
        fresh.extend(((a, b), each) for (a, b, each), when in groups_of.items() if when == turn)
        arrive(ext.at[pl.ds(0, len(queues) * UNIT)], turn)

    def tidy():
        for origin, sub in fresh:
            rim_leaves(origin, sub)
        for origin, sub in fresh:
            split_unit(base_of(origin, sub))
        fresh.clear()

    base = turns + SIDE

    def note_row(dx):
        return metas.at[lax.rem(x + dx + SIDE, SIDE), z]

    def note_column(dz):
        return metas.at[:, lax.rem(z + dz + SIDE, SIDE)]

    def note_wait(ref, k):
        arrive(ref, base + k)

    def bundle_of(slot, to):
        at = place(to)
        return helps.at[at // SIDE, :, 0] if slot == 0 else helps.at[:, lax.rem(at, SIDE), 1]

    def pair_of(slot, to, low):
        at = place(to)
        part = pl.ds(low, 2)
        return helps.at[at // SIDE, part, 0] if slot == 0 else helps.at[part, lax.rem(at, SIDE), 1]

    def final(slot, along, across):
        return arrived.at[slot, along % SIDE, across % SIDE - 1]

    passed, begun, turned, ended = base + 6, base + 7, base + 8, base + 9

    def target(slot, way):
        axis = 1 - slot
        at = place(step(axis, way))
        return lax.rem(at, SIDE) if axis == 1 else at // SIDE

    def far_pairs(slot):
        for way, low in ((1, 0), (-1, 2)):
            link.start(
                pair_of(slot, step(slot, 2), low), passing.at[slot, 0 if way > 0 else 1],
                HELPER, passed, neighbour(slot, way),
            )

    def bundle(slot):
        for way in (1, -1):
            link.start(
                bundle_of(slot, step(slot, way)), first.at[slot, -way % SIDE],
                HELPER, begun, neighbour(slot, way),
            )

    def relay(slot):
        for way, low in ((1, 0), (-1, 2)):
            link.start(
                passing.at[slot, 0 if way > 0 else 1], first.at[slot, 2, pl.ds(low, 2)],
                HELPER, begun, neighbour(slot, way),
            )

    def direct(slot, low):
        for way in (1, -1):
            link.start(
                first.at[slot, pl.ds(low, 2), target(slot, way)],
                arrived.at[slot, pl.ds(low, 2), -way % SIDE - 1],
                HELPER, ended + low // 2, neighbour(1 - slot, way),
            )

    by = {0: 1, 1: 1, 3: -1, 2: -1}
    soon = (0, 3)

    def detour(slot, low):
        link.start(
            first.at[slot, pl.ds(low, 2), target(slot, 2)], second.at[slot, pl.ds(low, 2)],
            HELPER, turned, neighbour(1 - slot, by[low]),
        )

    def hand_on(slot, along):
        link.start(
            second.at[slot, along], final(slot, along, 2),
            HELPER, ended + (2 if along in soon else 3), neighbour(1 - slot, by[along]),
        )

    slots = (0, 1)
    early = len(HELP_ORDER) - LATE

    def rim(has, start):
        @pl.when(has)
        def _():
            rim_whole(start == 0).wait_recv()
            for k in range(RIM // UNIT):
                split_unit(start + k * UNIT)

        @pl.when(jnp.logical_not(has))
        def _():
            ext_parts[start : start + RIM] = jnp.zeros((RIM,) + ext_parts.shape[1:], jnp.bfloat16)

    def noted(k, slot):
        along, across = HELP_ORDER[k]
        dx, dz = (along, across) if slot == 0 else (across, along)
        sx, sz = lax.rem(x + dx, SIDE), lax.rem(z + dz, SIDE)
        return [notes[sx, sz, kind, 0, n * 2 + slot] for kind in range(3)]

    def list_rows(low, high, lines, k):
        spots = lax.broadcasted_iota(jnp.int32, (1, terms.shape[0]), 1)
        rows, load = jnp.full_like(spots, blocks), jnp.zeros_like(spots)
        for each in range(low, high):
            for slot in slots:
                col, row, live = noted(each, slot)
                here = spots == (each - low) * 2 + slot
                rows = jnp.where(here, row, rows)
                load = jnp.where(here, col * 2 + live, load)
        order_table(load, rows, table)
        return fetch(table, lines, k)

    for turn in range(turns):
        for axis, way, queue, _ in queues:
            origin, sub = queue[turn]
            need(origin, sub)
            link.start(
                quarter(origin, sub) if any(origin) else sims.at[pl.ds(sub * UNIT, UNIT)],
                quarter(origin, sub),
                GATHER,
                turn,
                neighbour(axis, way),
            )
        if turn == 0:
            mine = fetch(sims, ext.at[pl.ds(RIM + n * blocks, blocks)], 0)
            told = [
                fetch(ref, metas.at[x, z, k], 1 + k)
                for k, ref in enumerate((help_cols, help_rows, help_live))
            ]
            vectors = [fetch(own_cols, vec.at[0], 6), fetch(own_rows, vec.at[1], 7)]
            for chunk in (0, 1):
                load(chunk).start()
            bundles = [
                fetch(helps.at[x, :, 0], first.at[0, 0], 4),
                fetch(helps.at[:, z, 1], first.at[1, 0], 5),
            ]
        if turn == 2:
            for copy in told:
                copy.wait()
            link.start(note_row(0), note_row(0), NOTES, base + 0, neighbour(0, 1))
            link.start(note_row(0), note_row(0), NOTES, base + 1, neighbour(0, -1))
            mine.wait()
        if turn == 4:
            note_wait(note_row(-1), 0)
            note_wait(note_row(1), 1)
            link.start(note_row(-1), note_row(-1), NOTES, base + 2, neighbour(0, 1))
        if turn == 7:
            note_wait(note_row(2), 2)
            link.start(note_column(0), note_column(0), NOTES + 1, base + 3, neighbour(1, 1))
            link.start(note_column(0), note_column(0), NOTES + 1, base + 4, neighbour(1, -1))
        for slot in slots:
            if turn == 3:
                far_pairs(slot)
            if turn == 6:
                if slot == 0:
                    arrive(passing, passed)
                relay(slot)
            if turn == 8:
                bundle(slot)
        if turn < 2:
            continue
        tidy()
        if turn == 2:
            for copy in vectors:
                copy.wait()
            order_table(vec[0], vec[1], table)
            fetch(table, order, 6).wait()
        chunks, spread = n_own // UNIT, turns - 2
        split_tiles(chunks * (turn - 2) // spread, chunks * (turn - 1) // spread)
    note_wait(note_column(-1), 3)
    note_wait(note_column(1), 4)
    link.start(note_column(-1), note_column(-1), NOTES + 1, base + 5, neighbour(1, 1))

    for axis, way, _, sub in queues:
        for across in range(SIDE):
            need((-way, across) if axis == 0 else (across, -way), sub)

    def ahead(axis, k):
        lead = SIDE - 1 - z if axis == 0 else SIDE - x
        return lax.rem(lead + k, SIDE)

    for k in range(SIDE):
        for axis, way, _, sub in queues:
            across = ahead(axis, k)
            origin = (-way, across) if axis == 0 else (across, -way)
            link.start(
                quarter(origin, sub), quarter(origin, sub), GATHER, turns + k, neighbour(axis, way)
            )
    for a in range(SIDE):
        for b in range(SIDE):
            for sub in range(4):
                if not (a == 2 and sub >= 2 or b == 2 and sub < 2):
                    need((a, b), sub)
    tidy()
    for copy in bundles:
        copy.wait()

    arrive(first.at[:, pl.ds(1, SIDE - 1)], begun)
    for low in (0, 2):
        for slot in slots:
            detour(slot, low)
    for low in (0, 2):
        for slot in slots:
            direct(slot, low)
    note_wait(note_column(2), 5)
    fetch(metas, notes, 1).wait()

    for k in range(SIDE):
        for axis, way, _, sub in queues:
            across = ahead(axis, k)
            origin = (2, across) if axis == 0 else (across, 2)
            fresh.append((origin, sub))
        arrive(ext.at[pl.ds(0, len(queues) * UNIT)], turns + k)
        tidy()
        if k == 0:
            help_table = list_rows(0, early, help_order, 2)
        if k == 1:
            help_table.wait()
            late_table = list_rows(early, len(HELP_ORDER), late_order, 3)
    rim(g > 0, 0)
    rim(g < groups - 1, total - RIM)
    link.whole(ext.at[pl.ds(0, len(queues) * (turns + SIDE) * UNIT)], GATHER, 0, neighbour(0, 1)).wait_send()

    @pl.when(g < groups - 1)
    def _():
        rim_whole(True).wait_send()

    @pl.when(g > 0)
    def _():
        rim_whole(False).wait_send()

    def own(low, high):
        def body(k, acc):
            for u in range(UNROLL):
                at = low + k * UNROLL + u
                keep = order[2, at].astype(jnp.float32)
                acc = acc * keep + product(tile_parts[order[0, at]], ext_parts[order[1, at]])
                ext[at] = acc
            return acc

        acc = jnp.zeros(ext.shape[1:], jnp.float32) if low == 0 else ext[low - 1]
        lax.fori_loop(0, (high - low) // UNROLL, body, acc)

    def help_products(low, high):
        for k in range(low, high):
            along, across = HELP_ORDER[k]
            for slot in slots:
                tile = (
                    arrived[slot, along, across - 1]
                    if across
                    else first[slot, along, target(slot, 0)]
                )
                terms[k * 2 + slot] = product(split(tile), ext_parts[noted(k, slot)[0]])

    cut = n_own // 2
    own(0, cut)
    arrive(second, turned)
    for part in (soon, (1, 2)):
        for along in part:
            for slot in slots:
                hand_on(slot, along)
    own(cut, n_own)

    @pl.loop(0, blocks)
    def _(row):
        sums[row] = ext[order[3, row]] * order[4, row].astype(jnp.float32)

    help_products(0, 4)
    arrive(first.at[0, pl.ds(0, 2)], ended)
    help_products(4, 8)
    arrive(first.at[0, pl.ds(0, 2)], ended + 1)
    help_products(8, 12)
    arrive(second.at[0], ended + 2)
    help_products(12, early)
    acc = jnp.zeros(ext.shape[1:], jnp.float32)
    for at in range(2 * early):
        keep = help_order[2, at].astype(jnp.float32)
        live = jnp.bitwise_and(help_order[1, at], 1).astype(jnp.float32)
        acc = acc * keep + terms[help_order[0, at]] * live
        ext[at] = acc

    @pl.loop(0, blocks)
    def _(row):
        sums[row] += ext[help_order[3, row]] * help_order[4, row].astype(jnp.float32)

    late_table.wait()
    link.whole(metas.at[0, pl.ds(0, 3)], NOTES, 0, neighbour(0, 1)).wait_send()
    link.whole(metas.at[pl.ds(0, 3)], NOTES + 1, 0, neighbour(0, 1)).wait_send()
    arrive(second.at[0], ended + 3)
    acc = jnp.zeros(ext.shape[1:], jnp.float32)
    for at in range(2 * LATE):
        which, load = late_order[0, at], late_order[1, at]
        tile = arrived[lax.rem(which, 2), 1 + which // 2, 1]
        keep = late_order[2, at].astype(jnp.float32)
        live = jnp.bitwise_and(load, 1).astype(jnp.float32)
        acc = acc * keep + product(split(tile), ext_parts[jnp.right_shift(load, 1)]) * live
        ext[at] = acc

    @pl.loop(0, blocks)
    def _(row):
        sums_out[row] = sums[row] + ext[late_order[3, row]] * late_order[4, row].astype(jnp.float32)

    link.whole(ext.at[pl.ds(0, 2 * helps_dev)], HELPER, 0, neighbour(0, 1)).wait_send()


def local(sims, own_tiles, own_cols, own_rows, help_tiles, help_cols, help_rows, help_live):
    blocks, size = sims.shape[0], sims.shape[1:]
    neighbours = lax.axis_size("nbr")
    helps, owns = help_tiles.shape[0], own_tiles.shape[0]
    extended = blocks * neighbours + 2 * RIM
    parts = (size[0], 2 * size[1])
    any_space = pl.BlockSpec(memory_space=pl.ANY)
    f32, bf16, i32 = jnp.float32, jnp.bfloat16, jnp.int32
    return pl.pallas_call(
        exchange,
        out_shape=pltpu.VMEM(sims.shape, f32),
        in_specs=[any_space] * 8,
        out_specs=pl.BlockSpec(memory_space=pltpu.VMEM),
        scratch_shapes=[
            pltpu.VMEM((extended,) + size, f32),
            pltpu.VMEM((extended,) + parts, bf16),
            pltpu.VMEM((owns,) + parts, bf16),
            pltpu.VMEM((2, UNIT) + size, f32),
            pltpu.VMEM((2, SIDE, SIDE) + size, f32),
            pltpu.VMEM((2, 2, 2) + size, f32),
            pltpu.VMEM((2, SIDE) + size, f32),
            pltpu.VMEM((2, SIDE, SIDE - 1) + size, f32),
            pltpu.VMEM((helps,) + size, f32),
            pltpu.VMEM(sims.shape, f32),
            pltpu.VMEM((SIDE, SIDE, 3, 1, helps), i32),
            pltpu.VMEM((2, 1, owns), i32),
            pltpu.VMEM((8, 256), i32),
            pltpu.SMEM((8, 256), i32),
            pltpu.SMEM((8, 256), i32),
            pltpu.SMEM((8, 256), i32),
            pltpu.SMEM((SIDE, SIDE, 3, 1, helps), i32),
            pltpu.SemaphoreType.DMA((4,)),
            pltpu.SemaphoreType.DMA((28,)),
            pltpu.SemaphoreType.DMA((2,)),
            pltpu.SemaphoreType.DMA((2,)),
            pltpu.SemaphoreType.DMA((8,)),
            pltpu.SemaphoreType.DMA((2,)),
        ],
        compiler_params=pltpu.CompilerParams(
            collective_id=0, has_side_effects=True, vmem_limit_bytes=57 * 2**20
        ),
        name="exchange",
    )(
        sims,
        help_tiles.reshape((SIDE, SIDE, 2) + size),
        own_tiles,
        *(v.reshape(1, -1) for v in (own_cols, own_rows, help_cols, help_rows, help_live)),
    )


def solution(mesh):
    whole, flat = P(("grp", "nbr"), None, None), P(("grp", "nbr"))
    placed = (whole, whole, flat, flat, whole, flat, flat, flat)
    return jax.shard_map(local, mesh=mesh, in_specs=placed, out_specs=whole, check_vma=False)
```

```python
import jax
import jax.numpy as jnp
from jax import lax
from jax.experimental import pallas as pl
from jax.experimental.pallas import tpu as pltpu
from jax.sharding import PartitionSpec as P

RIM = 8
UNIT = 4
SIDE = 4
UNROLL = 16
MESH = pl.DeviceIdType.MESH
GATHER, HELPER, NOTES = 0, 1, 2


def wrap(value):
    return (value + SIDE) % SIDE if isinstance(value, int) else lax.rem(value + SIDE, SIDE)


def gather_queues():
    queues = []
    for axis in (0, 1):
        for way in (1, -1):
            near, far = ((0, 1), (2, 3)) if axis == 0 else ((2, 3), (0, 1))
            if way < 0:
                near, far = near[::-1], far[::-1]

            def at(along, across, axis=axis):
                return (along, across) if axis == 0 else (across, along)

            queue = [
                (at(0, 0), near[0]),
                (at(0, 0), near[1]),
                (at(0, 0), far[0]),
                (at(-way, 0), near[0]),
                (at(0, 0), far[1]),
                (at(0, -1), far[0]),
                (at(0, 1), far[0]),
                (at(0, -1), far[1]),
                (at(0, 1), far[1]),
                (at(0, 2), far[0]),
                (at(0, 2), far[1]),
            ]
            queues.append((axis, way, queue, far[0]))
    return queues


class Link:
    def __init__(self, send, recv):
        self.send, self.recv = send, recv

    def start(self, src, dst, sent, arrival, device):
        pltpu.make_async_remote_copy(
            src_ref=src,
            dst_ref=dst,
            send_sem=self.send.at[sent],
            recv_sem=self.recv.at[arrival],
            device_id=device,
            device_id_type=MESH,
        ).start()

    def whole(self, ref, sent, arrival, device):
        return pltpu.make_async_remote_copy(
            src_ref=ref,
            dst_ref=ref,
            send_sem=self.send.at[sent],
            recv_sem=self.recv.at[arrival],
            device_id=device,
            device_id_type=MESH,
        )


def split(value):
    high = value.astype(jnp.bfloat16)
    low = (value - high.astype(jnp.float32)).astype(jnp.bfloat16)
    return jnp.concatenate([high, low], axis=1)


def product(tile, block):
    both = jnp.dot(
        tile, jnp.concatenate([block, block], axis=0), preferred_element_type=jnp.float32
    )
    half = both.shape[1] // 2
    return both[:, :half] + both[:, half:]


def order_table(cols, rows, table):
    count = rows.shape[1]
    table[...] = jnp.zeros_like(table)
    line = lax.broadcasted_iota(jnp.int32, (count, count), 1)
    deep = lax.broadcasted_iota(jnp.int32, (count, count), 0)

    def upright(value):
        return jnp.sum(jnp.where(line == deep, value, 0), axis=1, keepdims=True)

    key = rows * 256 + line[:1]
    key_up, col_up = upright(key), upright(cols)
    row_up = jnp.right_shift(key_up, 8)
    rank = jnp.sum((key < key_up).astype(jnp.int32), axis=1, keepdims=True)
    here = rank == line
    before = rank == line - 1
    row_at = jnp.sum(jnp.where(here, row_up, 0), axis=0, keepdims=True)
    row_before = jnp.sum(jnp.where(before, row_up + 1, 0), axis=0, keepdims=True) - 1
    table[0:1, :count] = jnp.sum(jnp.where(here, deep, 0), axis=0, keepdims=True)
    table[1:2, :count] = jnp.sum(jnp.where(here, col_up, 0), axis=0, keepdims=True)
    table[2:3, :count] = (row_at == row_before).astype(jnp.int32)
    upto = jnp.sum((row_up <= line).astype(jnp.int32), axis=0, keepdims=True)
    table[3:4, :count] = jnp.maximum(upto - 1, 0)
    table[4:5, :count] = jnp.minimum(
        jnp.sum((row_up == line).astype(jnp.int32), axis=0, keepdims=True), 1
    )


HELP_ORDER = (
    [(0, 0), (1, 0), (3, 0), (2, 0), (0, 1), (0, 3), (1, 1), (1, 3)]
    + [(3, 1), (3, 3), (2, 1), (2, 3), (0, 2), (3, 2), (1, 2), (2, 2)]
)
LATE = 2


def exchange(
    sims, helps, tiles, own_cols, own_rows, help_cols, help_rows, help_live,
    sums_out,
    ext, ext_parts, tile_parts, stage, first, passing, second, arrived, terms, sums,
    metas, vec, table, order, help_order, late_order, notes,
    send, recv, rim_send, rim_recv, local_sem, stage_sem,
):
    n, g = lax.axis_index("nbr"), lax.axis_index("grp")
    groups = lax.axis_size("grp")
    x, z = n // SIDE, lax.rem(n, SIDE)
    blocks = sims.shape[0]
    total = ext.shape[0]
    n_own = tiles.shape[0]
    last = SIDE * SIDE - 1
    helps_dev = terms.shape[0]

    def place(origin):
        return lax.rem(x + origin[0] + SIDE, SIDE) * SIDE + lax.rem(z + origin[1] + SIDE, SIDE)

    def step(axis, way):
        return (way, 0) if axis == 0 else (0, way)

    def neighbour(axis, way):
        return {"nbr": place(step(axis, way))}

    barrier = pltpu.get_barrier_semaphore()
    for axis in (0, 1):
        for way in (1, -1):
            pl.semaphore_signal(barrier, inc=1, device_id=neighbour(axis, way), device_id_type=MESH)

    @pl.when(g > 0)
    def _():
        pl.semaphore_signal(barrier, inc=1, device_id={"grp": g - 1}, device_id_type=MESH)

    @pl.when(g < groups - 1)
    def _():
        pl.semaphore_signal(barrier, inc=1, device_id={"grp": g + 1}, device_id_type=MESH)

    def fetch(src, dst, k):
        copy = pltpu.make_async_copy(src, dst, local_sem.at[k])
        copy.start()
        return copy

    def load(chunk):
        at = lax.rem(chunk, 2)
        return pltpu.make_async_copy(
            tiles.at[pl.ds(chunk * UNIT, UNIT)], stage.at[at], stage_sem.at[at]
        )

    pl.semaphore_wait(
        barrier, 4 + (g > 0).astype(jnp.int32) + (g < groups - 1).astype(jnp.int32)
    )
    link = Link(send, recv)

    def split_unit(start):
        @pl.loop(0, UNIT)
        def _(k):
            ext_parts[start + k] = split(ext[start + k])

    def split_tiles(low, high):
        @pl.loop(low, high)
        def _(chunk):
            load(chunk).wait()
            at = lax.rem(chunk, 2)

            @pl.loop(0, UNIT)
            def _(k):
                tile_parts[chunk * UNIT + k] = split(stage[at, k])

            @pl.when(chunk + 2 < n_own // UNIT)
            def _():
                load(chunk + 2).start()

    def rim_copy(piece):
        up = piece < 2
        src = total - 2 * RIM + piece * UNIT if up else RIM + (piece - 2) * UNIT
        dst = piece * UNIT if up else total - RIM + (piece - 2) * UNIT
        peer = lax.rem(g + 1, groups) if up else lax.rem(g + groups - 1, groups)
        return pltpu.make_async_remote_copy(
            src_ref=ext.at[pl.ds(src, UNIT)], dst_ref=ext.at[pl.ds(dst, UNIT)],
            send_sem=rim_send.at[piece // 2], recv_sem=rim_recv.at[piece // 2],
            device_id={"grp": peer}, device_id_type=MESH,
        )

    def rim_whole(up):
        ref = ext.at[pl.ds(0 if up else total - RIM, RIM)]
        return pltpu.make_async_remote_copy(
            src_ref=ref, dst_ref=ref,
            send_sem=rim_send.at[0 if up else 1], recv_sem=rim_recv.at[0 if up else 1],
            device_id=neighbour(0, 1), device_id_type=MESH,
        )

    def rim_leaves(origin, sub):
        at = place(origin)
        sends = (at == last) & (g < groups - 1) if sub >= 2 else (at == 0) & (g > 0)

        @pl.when(sends)
        def _():
            rim_copy(sub - 2 if sub >= 2 else sub + 2).start()

    def base_of(origin, sub):
        return RIM + place(origin) * blocks + sub * UNIT

    def quarter(origin, sub):
        return ext.at[pl.ds(base_of(origin, sub), UNIT)]

    queues = gather_queues()
    turns = len(queues[0][2])
    groups_of = {}
    for axis, way, queue, _ in queues:
        for turn, (origin, sub) in enumerate(queue):
            dx, dz = step(axis, way)
            groups_of[wrap(origin[0] - dx), wrap(origin[1] - dz), sub] = turn
    here = set()
    fresh = [((0, 0), sub) for sub in range(4)]

    def arrive(ref, arrival):
        link.whole(ref, 0, arrival, neighbour(0, 1)).wait_recv()

    def need(origin, sub):
        turn = groups_of.get((wrap(origin[0]), wrap(origin[1]), sub))
        if turn is None or turn in here:
            return
        here.add(turn)
        fresh.extend(((a, b), each) for (a, b, each), when in groups_of.items() if when == turn)
        arrive(ext.at[pl.ds(0, len(queues) * UNIT)], turn)

    def tidy():
        for origin, sub in fresh:
            rim_leaves(origin, sub)
        for origin, sub in fresh:
            split_unit(base_of(origin, sub))
        fresh.clear()

    base = turns + SIDE

    def note_row(dx):
        return metas.at[lax.rem(x + dx + SIDE, SIDE), z]

    def note_column(dz):
        return metas.at[:, lax.rem(z + dz + SIDE, SIDE)]

    def note_wait(ref, k):
        arrive(ref, base + k)

    def bundle_of(slot, to):
        at = place(to)
        return helps.at[at // SIDE, :, 0] if slot == 0 else helps.at[:, lax.rem(at, SIDE), 1]

    def pair_of(slot, to, low):
        at = place(to)
        part = pl.ds(low, 2)
        return helps.at[at // SIDE, part, 0] if slot == 0 else helps.at[part, lax.rem(at, SIDE), 1]

    def final(slot, along, across):
        return arrived.at[slot, along % SIDE, across % SIDE - 1]

    passed, begun, turned, ended = base + 6, base + 7, base + 8, base + 9

    def target(slot, way):
        axis = 1 - slot
        at = place(step(axis, way))
        return lax.rem(at, SIDE) if axis == 1 else at // SIDE

    def far_pairs(slot):
        for way, low in ((1, 0), (-1, 2)):
            link.start(
                pair_of(slot, step(slot, 2), low), passing.at[slot, 0 if way > 0 else 1],
                HELPER, passed, neighbour(slot, way),
            )

    def bundle(slot):
        for way in (1, -1):
            link.start(
                bundle_of(slot, step(slot, way)), first.at[slot, -way % SIDE],
                HELPER, begun, neighbour(slot, way),
            )

    def relay(slot):
        for way, low in ((1, 0), (-1, 2)):
            link.start(
                passing.at[slot, 0 if way > 0 else 1], first.at[slot, 2, pl.ds(low, 2)],
                HELPER, begun, neighbour(slot, way),
            )

    def direct(slot, low):
        for way in (1, -1):
            link.start(
                first.at[slot, pl.ds(low, 2), target(slot, way)],
                arrived.at[slot, pl.ds(low, 2), -way % SIDE - 1],
                HELPER, ended + low // 2, neighbour(1 - slot, way),
            )

    by = {0: 1, 1: 1, 3: -1, 2: -1}
    soon = (0, 3)

    def detour(slot, low):
        link.start(
            first.at[slot, pl.ds(low, 2), target(slot, 2)], second.at[slot, pl.ds(low, 2)],
            HELPER, turned, neighbour(1 - slot, by[low]),
        )

    def hand_on(slot, along):
        link.start(
            second.at[slot, along], final(slot, along, 2),
            HELPER, ended + (2 if along in soon else 3), neighbour(1 - slot, by[along]),
        )

    slots = (0, 1)
    early = len(HELP_ORDER) - LATE

    def rim(has, start):
        @pl.when(has)
        def _():
            rim_whole(start == 0).wait_recv()
            for k in range(RIM // UNIT):
                split_unit(start + k * UNIT)

        @pl.when(jnp.logical_not(has))
        def _():
            ext_parts[start : start + RIM] = jnp.zeros((RIM,) + ext_parts.shape[1:], jnp.bfloat16)

    def noted(k, slot):
        along, across = HELP_ORDER[k]
        dx, dz = (along, across) if slot == 0 else (across, along)
        sx, sz = lax.rem(x + dx, SIDE), lax.rem(z + dz, SIDE)
        return [notes[sx, sz, kind, 0, n * 2 + slot] for kind in range(3)]

    def list_rows(low, high, lines, k):
        spots = lax.broadcasted_iota(jnp.int32, (1, terms.shape[0]), 1)
        rows, load = jnp.full_like(spots, blocks), jnp.zeros_like(spots)
        for each in range(low, high):
            for slot in slots:
                col, row, live = noted(each, slot)
                here = spots == (each - low) * 2 + slot
                rows = jnp.where(here, row, rows)
                load = jnp.where(here, col * 2 + live, load)
        order_table(load, rows, table)
        return fetch(table, lines, k)

    for turn in range(turns):
        for axis, way, queue, _ in queues:
            origin, sub = queue[turn]
            need(origin, sub)
            link.start(
                quarter(origin, sub) if any(origin) else sims.at[pl.ds(sub * UNIT, UNIT)],
                quarter(origin, sub),
                GATHER,
                turn,
                neighbour(axis, way),
            )
        if turn == 0:
            mine = fetch(sims, ext.at[pl.ds(RIM + n * blocks, blocks)], 0)
            told = [
                fetch(ref, metas.at[x, z, k], 1 + k)
                for k, ref in enumerate((help_cols, help_rows, help_live))
            ]
            vectors = [fetch(own_cols, vec.at[0], 6), fetch(own_rows, vec.at[1], 7)]
            for chunk in (0, 1):
                load(chunk).start()
            bundles = [
                fetch(helps.at[x, :, 0], first.at[0, 0], 4),
                fetch(helps.at[:, z, 1], first.at[1, 0], 5),
            ]
        if turn == 2:
            for copy in told:
                copy.wait()
            link.start(note_row(0), note_row(0), NOTES, base + 0, neighbour(0, 1))
            link.start(note_row(0), note_row(0), NOTES, base + 1, neighbour(0, -1))
            mine.wait()
        if turn == 4:
            note_wait(note_row(-1), 0)
            note_wait(note_row(1), 1)
            link.start(note_row(-1), note_row(-1), NOTES, base + 2, neighbour(0, 1))
        if turn == 7:
            note_wait(note_row(2), 2)
            link.start(note_column(0), note_column(0), NOTES + 1, base + 3, neighbour(1, 1))
            link.start(note_column(0), note_column(0), NOTES + 1, base + 4, neighbour(1, -1))
        for slot in slots:
            if turn == 3:
                far_pairs(slot)
            if turn == 6:
                if slot == 0:
                    arrive(passing, passed)
                relay(slot)
            if turn == 8:
                bundle(slot)
        if turn < 2:
            continue
        tidy()
        if turn == 2:
            for copy in vectors:
                copy.wait()
            order_table(vec[0], vec[1], table)
            fetch(table, order, 6).wait()
        chunks, spread = n_own // UNIT, turns - 2
        split_tiles(chunks * (turn - 2) // spread, chunks * (turn - 1) // spread)
    note_wait(note_column(-1), 3)
    note_wait(note_column(1), 4)
    link.start(note_column(-1), note_column(-1), NOTES + 1, base + 5, neighbour(1, 1))

    for axis, way, _, sub in queues:
        for across in range(SIDE):
            need((-way, across) if axis == 0 else (across, -way), sub)

    def ahead(axis, k):
        lead = SIDE - 1 - z if axis == 0 else SIDE - x
        return lax.rem(lead + k, SIDE)

    for k in range(SIDE):
        for axis, way, _, sub in queues:
            across = ahead(axis, k)
            origin = (-way, across) if axis == 0 else (across, -way)
            link.start(
                quarter(origin, sub), quarter(origin, sub), GATHER, turns + k, neighbour(axis, way)
            )
    for a in range(SIDE):
        for b in range(SIDE):
            for sub in range(4):
                if not (a == 2 and sub >= 2 or b == 2 and sub < 2):
                    need((a, b), sub)
    tidy()
    for copy in bundles:
        copy.wait()

    arrive(first.at[:, pl.ds(1, SIDE - 1)], begun)
    for low in (0, 2):
        for slot in slots:
            detour(slot, low)
    for low in (0, 2):
        for slot in slots:
            direct(slot, low)
    note_wait(note_column(2), 5)
    fetch(metas, notes, 1).wait()

    for k in range(SIDE):
        for axis, way, _, sub in queues:
            across = ahead(axis, k)
            origin = (2, across) if axis == 0 else (across, 2)
            fresh.append((origin, sub))
        arrive(ext.at[pl.ds(0, len(queues) * UNIT)], turns + k)
        tidy()
        if k == 0:
            help_table = list_rows(0, early, help_order, 2)
        if k == 1:
            help_table.wait()
            late_table = list_rows(early, len(HELP_ORDER), late_order, 3)
    rim(g > 0, 0)
    rim(g < groups - 1, total - RIM)
    link.whole(ext.at[pl.ds(0, len(queues) * (turns + SIDE) * UNIT)], GATHER, 0, neighbour(0, 1)).wait_send()

    @pl.when(g < groups - 1)
    def _():
        rim_whole(True).wait_send()

    @pl.when(g > 0)
    def _():
        rim_whole(False).wait_send()

    def own(low, high):
        def body(k, acc):
            for u in range(UNROLL):
                at = low + k * UNROLL + u
                keep = order[2, at].astype(jnp.float32)
                acc = acc * keep + product(tile_parts[order[0, at]], ext_parts[order[1, at]])
                ext[at] = acc
            return acc

        acc = jnp.zeros(ext.shape[1:], jnp.float32) if low == 0 else ext[low - 1]
        lax.fori_loop(0, (high - low) // UNROLL, body, acc)

    def help_products(low, high):
        for k in range(low, high):
            along, across = HELP_ORDER[k]
            for slot in slots:
                tile = (
                    arrived[slot, along, across - 1]
                    if across
                    else first[slot, along, target(slot, 0)]
                )
                terms[k * 2 + slot] = product(split(tile), ext_parts[noted(k, slot)[0]])

    cut = n_own // 2
    own(0, cut)
    arrive(second, turned)
    for part in (soon, (1, 2)):
        for along in part:
            for slot in slots:
                hand_on(slot, along)
    own(cut, n_own)

    @pl.loop(0, blocks, unroll=4)
    def _(row):
        sums[row] = ext[order[3, row]] * order[4, row].astype(jnp.float32)

    help_products(0, 4)
    arrive(first.at[0, pl.ds(0, 2)], ended)
    help_products(4, 8)
    arrive(first.at[0, pl.ds(0, 2)], ended + 1)
    help_products(8, 12)
    arrive(second.at[0], ended + 2)
    help_products(12, early)
    acc = jnp.zeros(ext.shape[1:], jnp.float32)
    for at in range(2 * early):
        keep = help_order[2, at].astype(jnp.float32)
        live = jnp.bitwise_and(help_order[1, at], 1).astype(jnp.float32)
        acc = acc * keep + terms[help_order[0, at]] * live
        ext[at] = acc

    @pl.loop(0, blocks, unroll=4)
    def _(row):
        sums[row] += ext[help_order[3, row]] * help_order[4, row].astype(jnp.float32)

    late_table.wait()
    link.whole(metas.at[0, pl.ds(0, 3)], NOTES, 0, neighbour(0, 1)).wait_send()
    link.whole(metas.at[pl.ds(0, 3)], NOTES + 1, 0, neighbour(0, 1)).wait_send()
    arrive(second.at[0], ended + 3)
    acc = jnp.zeros(ext.shape[1:], jnp.float32)
    for at in range(2 * LATE):
        which, load = late_order[0, at], late_order[1, at]
        tile = arrived[lax.rem(which, 2), 1 + which // 2, 1]
        keep = late_order[2, at].astype(jnp.float32)
        live = jnp.bitwise_and(load, 1).astype(jnp.float32)
        acc = acc * keep + product(split(tile), ext_parts[jnp.right_shift(load, 1)]) * live
        ext[at] = acc

    @pl.loop(0, blocks, unroll=4)
    def _(row):
        sums_out[row] = sums[row] + ext[late_order[3, row]] * late_order[4, row].astype(jnp.float32)

    link.whole(ext.at[pl.ds(0, 2 * helps_dev)], HELPER, 0, neighbour(0, 1)).wait_send()


def local(sims, own_tiles, own_cols, own_rows, help_tiles, help_cols, help_rows, help_live):
    blocks, size = sims.shape[0], sims.shape[1:]
    neighbours = lax.axis_size("nbr")
    helps, owns = help_tiles.shape[0], own_tiles.shape[0]
    extended = blocks * neighbours + 2 * RIM
    parts = (size[0], 2 * size[1])
    any_space = pl.BlockSpec(memory_space=pl.ANY)
    f32, bf16, i32 = jnp.float32, jnp.bfloat16, jnp.int32
    return pl.pallas_call(
        exchange,
        out_shape=pltpu.VMEM(sims.shape, f32),
        in_specs=[any_space] * 8,
        out_specs=pl.BlockSpec(memory_space=pltpu.VMEM),
        scratch_shapes=[
            pltpu.VMEM((extended,) + size, f32),
            pltpu.VMEM((extended,) + parts, bf16),
            pltpu.VMEM((owns,) + parts, bf16),
            pltpu.VMEM((2, UNIT) + size, f32),
            pltpu.VMEM((2, SIDE, SIDE) + size, f32),
            pltpu.VMEM((2, 2, 2) + size, f32),
            pltpu.VMEM((2, SIDE) + size, f32),
            pltpu.VMEM((2, SIDE, SIDE - 1) + size, f32),
            pltpu.VMEM((helps,) + size, f32),
            pltpu.VMEM(sims.shape, f32),
            pltpu.VMEM((SIDE, SIDE, 3, 1, helps), i32),
            pltpu.VMEM((2, 1, owns), i32),
            pltpu.VMEM((8, 256), i32),
            pltpu.SMEM((8, 256), i32),
            pltpu.SMEM((8, 256), i32),
            pltpu.SMEM((8, 256), i32),
            pltpu.SMEM((SIDE, SIDE, 3, 1, helps), i32),
            pltpu.SemaphoreType.DMA((4,)),
            pltpu.SemaphoreType.DMA((28,)),
            pltpu.SemaphoreType.DMA((2,)),
            pltpu.SemaphoreType.DMA((2,)),
            pltpu.SemaphoreType.DMA((8,)),
            pltpu.SemaphoreType.DMA((2,)),
        ],
        compiler_params=pltpu.CompilerParams(
            collective_id=0, has_side_effects=True, vmem_limit_bytes=57 * 2**20
        ),
        name="exchange",
    )(
        sims,
        help_tiles.reshape((SIDE, SIDE, 2) + size),
        own_tiles,
        *(v.reshape(1, -1) for v in (own_cols, own_rows, help_cols, help_rows, help_live)),
    )


def solution(mesh):
    whole, flat = P(("grp", "nbr"), None, None), P(("grp", "nbr"))
    placed = (whole, whole, flat, flat, whole, flat, flat, flat)
    return jax.shard_map(local, mesh=mesh, in_specs=placed, out_specs=whole, check_vma=False)
```
